32 devices in a mesh: segment: 2 (over y), expert: 16 (over z, x, core).
Axes of the slice: x: 2, y: 2, z: 4, core: 2. Of those that a mesh axis runs over, the one named last changes fastest.
Arguments:
- hidden: bfloat16 [2, 512, 2048], P('segment', 'expert'), may hold values from -6 to 6
- memory: bfloat16 [2, 512, 2048], P('segment', 'expert'), may hold values from -6 to 6
- lengths: int32 [2, 16], P('segment', 'expert'), may hold values from 1 to 32, as said below
- memory_lengths: int32 [2, 16], P('segment', 'expert'), may hold values from 1 to 32, as said below
- routes: int32 [2, 512, 2], P('segment', 'expert'), may hold values from 0 to 3, all different within a row; in each aligned block of 32 rows (0 to 31, 32 to 63, ..., all dimensions but the last counted through in order) at most 20 rows name the same one
- norm_gain: float32 [2, 3, 2048], P('segment'), may hold values from 0.5 to 1.5, as said below
- router: bfloat16 [2, 2048, 4], P('segment'), may hold values from -0.26516504 to 0.26516504, as said below
- w_in: bfloat16 [2, 2048, 16384], P('segment', None, 'expert'), may hold values from -0.13258252 to 0.13258252, as said below
- w_out: bfloat16 [2, 16384, 2048], P('segment', 'expert'), may hold values from -0.125 to 0.125, as said below
- shortlist: bfloat16 [2, 2048, 512], P('segment'), may hold values from -0.375 to 0.375
- student: float32 [2, 512, 512], P('segment', 'expert'), may hold values from -15 to 15
- targets: int32 [2, 512], P('segment', 'expert'), may hold values from 0 to 511
Outputs:
- layer_out: bfloat16 [2, 512, 2048], P('segment', 'expert')
- loss: float32 [], replicated
The draws below stay inside these ranges and needn't reach their ends.
Inputs may be any that keep to these rules, and one draw needn't show every extreme that they name: `lengths`: every sequence has at least one position; the first sequence of each section has 32. `memory_lengths`: every sequence has at least one position; the first sequence of each section has 32. `routes`: A token's two experts differ. In the 32 rows of one device no expert is named more than 20 times, a bound that some block reaches. `norm_gain`: equal in all encoder sections, and equal in all decoder sections. `router`: equal in all encoder sections, and equal in all decoder sections. `w_in`: equal in all encoder sections, and equal in all decoder sections. `w_out`: equal in all encoder sections, and equal in all decoder sections.
All inputs are finite; a program needn't handle non-finite values.
Results may differ from the reference program's by a relative error of at most 0.0049.
Values may be sent and summed in bfloat16 or wider, within the bound.
A program may use at most 64 MiB of HBM per device.

```python
import math
import jax
import jax.numpy as jnp
import numpy as np
from jax import lax

D = 2048
HEADS = 16
HEAD_DIM = 128
FF = 4096
EXPERTS = 4
VOCW = 512
LEN = 32
TOK_DEV = 32
CAP = 20
SEQS = 16
TOKENS = 512
N_SEGMENT = 2
N_EXPERT = 16


def lengths_common(key):
    drawn = jax.random.randint(key, (N_SEGMENT, SEQS), 1, LEN + 1)
    return drawn.at[:, 0].set(LEN).astype(jnp.int32)


def draw_lengths(key, part):
    return lengths_common(jax.random.fold_in(key, 11))


def draw_memory_lengths(key, part):
    return lengths_common(jax.random.fold_in(key, 12))


def shared_sets(key, shape, scale, limit):
    drawn = jnp.clip(jax.random.normal(key, (2,) + shape, jnp.float32) * scale, -limit, limit)
    return jnp.repeat(drawn, N_SEGMENT // 2, axis=0)


def draw_norm_gain(key, part):
    spread = shared_sets(jax.random.fold_in(key, 21), (3, D), 0.1, 0.5)
    return (1.0 + spread).astype(jnp.float32)


def draw_router(key, part):
    return shared_sets(jax.random.fold_in(key, 22), (D, EXPERTS), 2.0 / math.sqrt(D), 12.0 / math.sqrt(D)).astype(jnp.bfloat16)


def draw_w_in(key, part):
    return shared_sets(jax.random.fold_in(key, 23), (D, EXPERTS * FF), 1.0 / math.sqrt(D), 6.0 / math.sqrt(D)).astype(jnp.bfloat16)


def draw_w_out(key, part):
    return shared_sets(jax.random.fold_in(key, 24), (EXPERTS * FF, D), math.sqrt(2.0 / FF), 8.0 / math.sqrt(FF)).astype(jnp.bfloat16)


def plant(values, rng, smallest, largest):
    longest = values.shape.index(max(values.shape))
    spots = []
    for shift in (0, 1):
        where = [jax.random.randint(jax.random.fold_in(rng, axis), (), 0, length) for axis, length in enumerate(values.shape)]
        where[longest] = (where[longest] + shift) % values.shape[longest]
        spots.append(tuple(where))
    return values.at[spots[0]].set(smallest).at[spots[1]].set(largest)


def shard_levels(rng, dims, pieces, low, top_value):
    def one(position, shards_of):
        steps = jax.random.uniform(jax.random.fold_in(jax.random.fold_in(rng, 6), position), (shards_of,), jnp.float32, low / len(pieces), top_value / len(pieces))
        return jnp.repeat(jnp.exp(steps), dims[position] // shards_of).reshape((-1,) + (1,) * (len(dims) - position - 1))

    level = one(*pieces[0])
    for cut in pieces[1:]:
        level = level * one(*cut)
    return level


def deal_out(own_key, own, number, rows, count, top, most, skew):
    order = jax.random.permutation(own_key, count)
    heavy_load, usual = portions_of(count, rows * top, most, skew, True), portions_of(count, rows * top, most, skew, False)
    places = jnp.arange(count)

    def named(sizes, offset_by):
        used = int((sizes > 0).sum())
        fixed = max(1, used // 4)
        shifted = fixed + (places - fixed + offset_by * (used - fixed)) % max(1, count - fixed)
        return jnp.zeros((count,), jnp.int32).at[order[jnp.where(places < fixed, places, shifted)]].set(jnp.asarray(sizes, jnp.int32))

    sizes = jnp.where(number % 4 == 0, named(heavy_load, number // 4), named(usual, number - number // 4 - 1))
    mixed = jax.random.permutation(jax.random.fold_in(own, 3), count)
    giver, taker = mixed[0:count // 2 * 2:2], mixed[1:count // 2 * 2:2]
    slack = jnp.minimum(sizes[giver] - 1, most - sizes[taker]) // 2
    slack = jnp.where((giver == order[0]) | (taker == order[0]) | (sizes[taker] == 0), 0, jnp.maximum(slack, 0))
    shifted = jax.random.randint(jax.random.fold_in(own, 4), (count // 2,), 0, 1 << 20) % (slack + 1)
    sizes = sizes.at[giver].add(-shifted).at[taker].add(shifted)
    items = jnp.searchsorted(jnp.cumsum(sizes), jnp.arange(rows * top), side="right").astype(jnp.int32)
    grid = items.reshape(top, rows).T
    grid = grid[jax.random.permutation(jax.random.fold_in(own, 1), rows)]
    offset_by = jax.random.randint(jax.random.fold_in(own, 2), (rows, 1), 0, top)
    return jnp.take_along_axis(grid, (jnp.arange(top)[None, :] + offset_by) % top, axis=1)


def portions_of(number_of, total, bound, lean, full):
    weights = [(1 << 20) // math.isqrt(standing ** lean) + 1 for standing in range(1, number_of + 1)]
    largest = bound if full else min(bound, max(-(-total // number_of), total * weights[0] // sum(weights)))
    least = 1 if total - largest >= number_of - 1 else 0
    given, surplus = [largest] + [least] * (number_of - 1), total - largest - least * (number_of - 1)
    while surplus > 0:
        movable = [i for i in range(1, number_of) if given[i] < largest] or [i for i in range(1, number_of) if given[i] < bound]
        pool, remaining = sum([weights[i] for i in movable]), surplus
        for i in movable:
            more = min(bound - given[i], max(1, remaining * weights[i] // pool), surplus)
            given[i] = given[i] + more
            surplus = surplus - more
    return np.array(given)


def noise(rng, shape, deviation, bound, pieces=(), held_as=jnp.bfloat16):
    loudness = shard_levels(rng, shape, pieces, -0.22, 0.18) if pieces else 1.0
    values = jax.random.normal(rng, shape, jnp.float32) * deviation * loudness
    return jnp.minimum(jnp.maximum(values, -bound), bound).astype(held_as)


def setup_inputs(seed: int = 0) -> dict:
    seeds = jax.random.split(jax.random.key(seed), 13)
    hidden = noise(seeds[0], (N_SEGMENT, TOKENS, D), 1.0, 6.0, ((0, 2), (1, 16)))
    memory = noise(seeds[1], (N_SEGMENT, TOKENS, D), 1.0, 6.0, ((0, 2), (1, 16)))
    lengths = draw_lengths(jax.random.fold_in(seeds[12], 71), 0)
    memory_lengths = draw_memory_lengths(jax.random.fold_in(seeds[12], 71), 0)
    routes_keys = jax.random.split(jax.random.fold_in(seeds[4], 1), N_SEGMENT * TOKENS // TOK_DEV)
    routes_turns = jax.random.permutation(jax.random.fold_in(seeds[4], 3), N_SEGMENT * TOKENS // TOK_DEV)
    routes = jax.vmap(lambda own, number: deal_out(jax.random.fold_in(seeds[4], 2), own, number, TOK_DEV, EXPERTS, 2, CAP, 2))(routes_keys, routes_turns).reshape((N_SEGMENT, TOKENS, 2))
    norm_gain = draw_norm_gain(jax.random.fold_in(seeds[12], 71), 0)
    router = draw_router(jax.random.fold_in(seeds[12], 71), 0)
    w_in = draw_w_in(jax.random.fold_in(seeds[12], 71), 0)
    w_out = draw_w_out(jax.random.fold_in(seeds[12], 71), 0)
    shortlist = noise(seeds[9], (N_SEGMENT, D, VOCW), (D // 9) ** -0.5, 0.375, ((0, 2),))
    student = noise(seeds[10], (N_SEGMENT, TOKENS, VOCW), 3.0, 15.0, ((0, 2), (1, 16)), jnp.float32)
    targets = plant(jax.random.randint(seeds[11], (N_SEGMENT, TOKENS), 0, VOCW), jax.random.fold_in(seeds[11], 1), 0, VOCW - 1).astype(jnp.int32)
    return {"hidden": hidden, "memory": memory, "lengths": lengths, "memory_lengths": memory_lengths, "routes": routes, "norm_gain": norm_gain, "router": router, "w_in": w_in, "w_out": w_out, "shortlist": shortlist, "student": student, "targets": targets}


epsilon = 1e-05

def layer_norm(values, gain_row):
    centred = values - lax.optimization_barrier(jnp.mean(values, axis=-1, keepdims=True))
    spread = lax.optimization_barrier(jnp.mean(centred * centred, axis=-1, keepdims=True))
    return centred * lax.rsqrt(spread + epsilon) * gain_row

def round_trip(values):
    return lax.optimization_barrier(values.astype(jnp.bfloat16)).astype(jnp.float32)

def reference(hidden, memory, lengths, memory_lengths, routes, norm_gain, router, w_in, w_out, shortlist, student, targets):
    half_segments = N_SEGMENT // 2
    group_size = N_EXPERT // EXPERTS
    part_width = FF // group_size
    tokens = hidden.shape[1]
    positions = jnp.arange(tokens) % LEN
    seq_index = jnp.arange(tokens) // LEN
    expert_ids = jnp.arange(EXPERTS)
    score_scale = 1.0 / math.sqrt(HEAD_DIM)
    outputs = []
    loss_sum = jnp.zeros((), jnp.float32)
    loss_count = jnp.zeros((), jnp.float32)
    for section in range(N_SEGMENT):
        states = hidden[section].astype(jnp.float32)
        is_valid = positions < lengths[section][seq_index]
        if section >= half_segments:
            source = section - half_segments
            key_rows = memory[source]
            allowed = positions < memory_lengths[source][seq_index]
            queries = layer_norm(states, norm_gain[section, 0]).astype(jnp.bfloat16)
            query_heads = queries.reshape(SEQS, LEN, HEADS, HEAD_DIM).astype(jnp.float32)
            key_heads = key_rows.reshape(SEQS, LEN, HEADS, HEAD_DIM).astype(jnp.float32)
            scores = jnp.einsum('bqhd,bkhd->bhqk', query_heads, key_heads) * score_scale
            scores = jnp.where(allowed.reshape(SEQS, 1, 1, LEN), scores, -1e+30)
            weights = round_trip(jax.nn.softmax(scores, axis=-1))
            attended = jnp.einsum('bhqk,bkhd->bqhd', weights, key_heads).reshape(tokens, D)
            mid_states = states + attended
        else:
            mid_states = states
        normed = layer_norm(mid_states, norm_gain[section, 1]).astype(jnp.bfloat16)
        router_probs = jax.nn.softmax(jnp.dot(normed, router[section], preferred_element_type=jnp.float32), axis=-1)
        first_hot = (routes[section][:, 0:1] == expert_ids).astype(jnp.float32)
        second = (routes[section][:, 1:2] == expert_ids).astype(jnp.float32)
        prob_first = lax.optimization_barrier(jnp.sum(router_probs * first_hot, axis=-1, keepdims=True))
        prob_second = lax.optimization_barrier(jnp.sum(router_probs * second, axis=-1, keepdims=True))
        prob_total = prob_first + prob_second
        gate_rows = (prob_first * first_hot + prob_second * second) / prob_total
        combine_rows = gate_rows * is_valid[:, None].astype(jnp.float32)
        first_stack = w_in[section].reshape(D, EXPERTS, FF).transpose(1, 0, 2)
        second_stack = w_out[section].reshape(EXPERTS, group_size, part_width, D)

        def expert_step(running, stacked):
            first_weight, second_weight, share_col = stacked
            activated = jnp.maximum(jnp.dot(normed, first_weight, preferred_element_type=jnp.float32), 0.0)
            activated = round_trip(activated).reshape(tokens, group_size, part_width)
            parts = jnp.einsum('tgf,gfd->tgd', activated, second_weight.astype(jnp.float32))
            parts = round_trip(parts)
            return (running + share_col[:, None] * lax.optimization_barrier(jnp.sum(parts, axis=1)), None)
        moe_out, _ = lax.scan(expert_step, jnp.zeros((tokens, D), jnp.float32), (first_stack, second_stack, combine_rows.T))
        layer_out = (mid_states + moe_out).astype(jnp.bfloat16)
        outputs.append(layer_out)
        if section >= half_segments:
            final_normed = layer_norm(layer_out.astype(jnp.float32), norm_gain[section, 2]).astype(jnp.bfloat16)
            teacher = jax.nn.log_softmax(jnp.dot(final_normed, shortlist[section], preferred_element_type=jnp.float32), axis=-1)
            learner = jax.nn.log_softmax(student[section], axis=-1)
            picked = (targets[section][:, None] == jnp.arange(VOCW)).astype(jnp.float32)
            token_loss = lax.optimization_barrier(jnp.sum(jnp.exp(teacher) * (teacher - learner), axis=-1)) - lax.optimization_barrier(jnp.sum(picked * learner, axis=-1))
            counted = is_valid.astype(jnp.float32)
            loss_sum = loss_sum + jnp.sum(token_loss * counted)
            loss_count = loss_count + jnp.sum(counted)
    return (jnp.stack(outputs), loss_sum / loss_count)
```

```python
import functools
import math

import jax
import jax.numpy as jnp
from jax import lax
from jax.experimental import pallas as pl
from jax.experimental.pallas import tpu as pltpu
from jax.sharding import PartitionSpec as P

HEAD_DIM = 128
LEN = 32
EPS = 1e-05
MESH = pl.DeviceIdType.MESH
BF = jnp.bfloat16
F32 = jnp.float32


def layer_norm(values, gain_row):
    centred = values - jnp.mean(values, axis=-1, keepdims=True)
    spread = jnp.mean(centred * centred, axis=-1, keepdims=True)
    return centred * lax.rsqrt(spread + EPS) * gain_row


def xor(a, k, count):
    out = 0
    bit = 1
    while bit < count:
        out = out + lax.rem(a // bit + (k // bit) % 2, 2) * bit
        bit *= 2
    return out


def kernel(
    n_seg, n_exp, experts, gx, gc,
    hidden_any, memory, lengths, memory_lengths, routes_any, gain_any, router_any,
    w_in, w_out, shortlist, student_any, targets,
    layer_out, loss_out,
    hidden, routes, norm_gain, router, student, out_stage,
    win, wout, short, kmem, klen_src, klen, mid,
    out_a, out_b, x, x_b, stage, act, y0,
    core, rc, xs_a, xs_b, rx_a, rx_b, zs_a, zs_b, z_a, z_b, z_all, z_stage,
    lsend, lrecv, lwide, tally,
    wsem, msem, ra, rb, rc_r, rx_r, rz_r, sent, l_s, l_r,
):
    seg = lax.axis_index("segment")
    me = lax.axis_index("expert")
    half_seg = n_seg // 2
    group = gx * gc
    e = me // group
    j = lax.rem(me, group)
    xi = j // gc
    ci = lax.rem(j, gc)
    tok = hidden.shape[1]
    width = hidden.shape[2]
    heads = width // HEAD_DIM
    cap = 5 * tok // 8
    main = cap // 16 * 16
    rest = cap - main
    hop_order = list(range(1, experts))

    def peer(ds, d):
        return (lax.rem(seg + ds, n_seg), lax.rem(me + d, n_exp))

    def dev(e2, x2, c2):
        return (seg, (e2 * gx + x2) * gc + c2)

    barrier = pltpu.get_barrier_semaphore()
    for ds in range(n_seg):
        for d in range(n_exp):
            if ds or d:
                pl.semaphore_signal(
                    barrier, inc=1, device_id=peer(ds, d), device_id_type=MESH
                )

    early = [
        pltpu.make_async_copy(hidden_any, hidden, wsem.at[3]),
        pltpu.make_async_copy(gain_any, norm_gain, wsem.at[4]),
        pltpu.make_async_copy(routes_any, routes, wsem.at[5]),
        pltpu.make_async_copy(router_any, router, wsem.at[6]),
        pltpu.make_async_copy(student_any, student, wsem.at[7]),
    ]
    for load in early:
        load.start()
    loads = [
        pltpu.make_async_copy(w_in.at[0], win, wsem.at[0]),
        pltpu.make_async_copy(w_out.at[0], wout, wsem.at[1]),
        pltpu.make_async_copy(shortlist.at[0], short, wsem.at[2]),
    ]
    for load in loads:
        load.start()

    klen_src[...] = jnp.broadcast_to(memory_lengths[0:1, 0:1], klen_src.shape)
    for q in range(1, tok // LEN):
        klen_src[q : q + 1, :] = jnp.broadcast_to(memory_lengths[0:1, q : q + 1], (1, 128))
    pl.semaphore_wait(barrier, n_exp * n_seg - 1)

    is_decoder = seg >= half_seg
    to_seg = lax.rem(seg + half_seg, n_seg)
    groups = 4
    band = width // groups
    mem_copies = [
        pltpu.make_async_remote_copy(
            memory.at[0, :, g * band : (g + 1) * band], kmem.at[:, g * band : (g + 1) * band],
            msem.at[2], msem.at[3 + g], device_id=(to_seg, me), device_id_type=MESH,
        )
        for g in range(groups)
    ]
    len_copy = pltpu.make_async_remote_copy(
        klen_src, klen, msem.at[0], msem.at[1], device_id=(to_seg, me), device_id_type=MESH
    )

    @pl.when(seg < half_seg)
    def _():
        len_copy.start()
        for copy in mem_copies:
            copy.start()

    early[0].wait()
    early[1].wait()
    gains = [norm_gain[i] for i in range(3)]
    states = hidden[0].astype(F32)

    @pl.when(seg < half_seg)
    def _():
        mid[...] = states

    @pl.when(seg >= half_seg)
    def _():
        queries = layer_norm(states, gains[0]).astype(BF)
        len_copy.wait_recv()
        col = lax.broadcasted_iota(jnp.int32, (tok, tok), 1)
        row = lax.broadcasted_iota(jnp.int32, (tok, tok), 0)
        klen_v = klen[...]
        allowed = jnp.zeros((tok, tok), jnp.bool_)
        for q in range(tok // LEN):
            inside = (col >= q * LEN) & (col - q * LEN < klen_v[q : q + 1, 0:1])
            inside = inside & (col < (q + 1) * LEN) & (row >= q * LEN) & (row < (q + 1) * LEN)
            allowed = allowed | inside
        for g in range(groups):
            mem_copies[g].wait_recv()
            keys = kmem[:, g * band : (g + 1) * band]
            parts = [slice(h * HEAD_DIM, (h + 1) * HEAD_DIM) for h in range(band // HEAD_DIM)]
            scores = jnp.concatenate(
                [
                    jnp.where(
                        allowed,
                        lax.dot_general(
                            queries[:, g * band + part.start : g * band + part.stop], keys[:, part],
                            (((1,), (1,)), ((), ())), preferred_element_type=F32,
                        )
                        * (1.0 / math.sqrt(HEAD_DIM)),
                        -1e30,
                    )
                    for part in parts
                ],
                axis=0,
            )
            top = jnp.max(scores, axis=-1, keepdims=True)
            raised = jnp.exp(scores - top)
            weights = (raised / jnp.sum(raised, axis=-1, keepdims=True)).astype(BF)
            for h, part in enumerate(parts):
                here = slice(g * band + part.start, g * band + part.stop)
                mid[:, here] = states[:, here] + jnp.dot(
                    weights[h * tok : (h + 1) * tok], keys[:, part], preferred_element_type=F32
                )

    normed = layer_norm(mid[...], gains[1]).astype(BF)

    early[2].wait()
    expert_lane = lax.broadcasted_iota(jnp.int32, (tok, experts), 1)
    pos = lax.broadcasted_iota(jnp.int32, (tok, 1), 0)
    valid = jnp.zeros((tok, 1), F32)
    for q in range(tok // LEN):
        ok = (pos >= q * LEN) & (pos < (q + 1) * LEN) & (pos - q * LEN < lengths[0:1, q : q + 1])
        valid = valid + ok.astype(F32)
    square = lax.broadcasted_iota(jnp.int32, (tok, tok), 0) == lax.broadcasted_iota(
        jnp.int32, (tok, tok), 1
    )

    def column(row):
        spread = jnp.where(square, jnp.broadcast_to(row, (tok, tok)), 0)
        return jnp.sum(spread.astype(F32), axis=-1, keepdims=True)

    expert_lane = expert_lane.astype(F32)
    first_hot = (column(routes[0, 0:1, :]) == expert_lane).astype(F32)
    second_hot = (column(routes[0, 1:2, :]) == expert_lane).astype(F32)
    chosen = (first_hot + second_hot) * valid
    before = (
        lax.broadcasted_iota(jnp.int32, (tok, tok), 1)
        < lax.broadcasted_iota(jnp.int32, (tok, tok), 0)
    ).astype(BF)
    rank = jnp.dot(before, chosen.astype(BF), preferred_element_type=F32)
    n_main = experts * main
    n_slots = experts * cap
    lanes = -(-n_slots // 128) * 128
    lane = lax.broadcasted_iota(jnp.int32, (1, lanes), 1)
    slot_of = jnp.full((1, lanes), -1, jnp.int32)
    expert_of = jnp.full((1, lanes), -1, jnp.int32)
    for k in range(experts):
        ek = xor(e, k, experts)
        in_main = (lane >= k * main) & (lane < (k + 1) * main)
        low = n_main + k * rest
        in_rest = (lane >= low) & (lane < low + rest)
        slot_of = jnp.where(in_main, lane - k * main, slot_of)
        slot_of = jnp.where(in_rest, lane - low + main, slot_of)
        expert_of = jnp.where(in_main | in_rest, ek, expert_of)
    placing = jnp.zeros((tok, lanes), F32)
    for k in range(experts):
        here = (expert_of == k) & (rank[:, k : k + 1] == slot_of.astype(F32))
        placing = placing + jnp.where(here, chosen[:, k : k + 1], 0.0)
    place_rows = jnp.transpose(placing)[0:n_slots].astype(BF)
    slots = jnp.dot(place_rows, normed, preferred_element_type=F32)

    chunk = gc * gx * cap
    side = gx * cap
    side_main = gx * main
    half_width = width // 2
    halves = [slice(h * half_width, (h + 1) * half_width) for h in range(2)]

    def rows_a(dc, dx, k):
        return pl.ds(k * chunk + dc * side + dx * main, main)

    def index_b(dc, dx, k):
        return (dc * gx + dx) * experts + k

    for k in hop_order:
        out_a[k] = slots[k * main : (k + 1) * main].astype(BF)
        out_b[k] = slots[n_main + k * rest : n_main + (k + 1) * rest].astype(BF)
    x[rows_a(0, 0, 0), :] = slots[0:main].astype(BF)
    x_b[0] = slots[n_main : n_main + rest].astype(BF)

    def send(src, dst, r_sem, target):
        pltpu.make_async_remote_copy(
            src, dst, sent, r_sem, device_id=target, device_id_type=MESH
        ).start()

    def landed(ref, sem):
        pltpu.make_async_copy(ref, ref, sem).wait()

    def count(size, sem):
        landed(tally.at[0 : size // 1024], sem)

    def piece(slot, p):
        if p < 2:
            return x.at[rows_a(*slot), halves[p]]
        return x_b.at[index_b(*slot)]

    def mark(slot, p):
        if slot[0]:
            return rb.at[slot[1] * experts + slot[2]]
        return ra.at[2 * (slot[1] * experts + slot[2]) + min(p, 1)]

    def arrived(slot, p):
        if p == 0:
            landed(piece(slot, 0), mark(slot, 0))
        elif p == 1:
            count(main * half_width + rest * width, mark(slot, 1))

    def forward(slot_from, slot_to, p, target):
        send(piece(slot_from, p), piece(slot_to, p), mark(slot_to, p), target)

    for k in hop_order:
        target = dev(xor(e, k, experts), xi, ci)
        for p in range(3):
            src = out_a.at[k, :, halves[p]] if p < 2 else out_b.at[k]
            send(src, piece((0, 0, k), p), mark((0, 0, k), p), target)

    core_dev = dev(e, xi, lax.rem(ci + 1, gc))

    def from_column(k):
        for p in range(3):
            if k:
                arrived((0, 0, k), p)
            for d in range(1, gx):
                forward((0, 0, k), (0, d, k), p, dev(e, lax.rem(xi + d, gx), ci))
            forward((0, 0, k), (1, 0, k), p, core_dev)

    def from_chips(k):
        for p in range(3):
            for d in range(1, gx):
                arrived((0, d, k), p)
                forward((0, d, k), (1, d, k), p, core_dev)

    units = win.shape[1]
    tile = min(512, units)
    tile2 = min(512, half_width)

    def first(k):
        for d in range(gx):
            count(cap * width, mark((1, d, k), 0))
        for dc in range(gc):
            for d in range(gx):
                stage[d * rest : (d + 1) * rest, :] = x_b[index_b(dc, d, k)].astype(F32)
            low = k * chunk + dc * side + side_main
            x[low : low + gx * rest, :] = stage[...].astype(BF)
        if k == 0:
            loads[0].wait()
        rows = slice(k * chunk, (k + 1) * chunk)

        @pl.loop(0, units // tile)
        def _(i):
            cols = pl.ds(pl.multiple_of(i * tile, tile), tile)
            act[:, cols] = jnp.maximum(
                jnp.dot(x[rows, :], win[:, cols], preferred_element_type=F32), 0.0
            ).astype(BF)

    def second(k):
        if k == 0:
            loads[1].wait()
        for h in range(2):
            @pl.loop(0, half_width // tile2)
            def _(i):
                cols = pl.ds(pl.multiple_of(h * half_width + i * tile2, tile2), tile2)
                part = jnp.dot(act[...], wout[:, cols], preferred_element_type=F32)
                core[k, :, cols] = part[side:].astype(BF)
                y0[k, :, cols] = part[0:side]

            send(core.at[k, :, halves[h]], rc.at[k, :, halves[h]], rc_r.at[2 * k + h], core_dev)

    def to_chips(k):
        for h in range(2):
            part = halves[h]
            landed(rc.at[k, :, part], rc_r.at[2 * k + h])
            tail = y0[k, side_main:, part] + rc[k, side_main:, part].astype(F32)
            for d in range(1, gx):
                o = (d - 1) * experts + k
                rows = slice(d * main, (d + 1) * main)
                xs_a[o, :, part] = (y0[k, rows, part] + rc[k, rows, part].astype(F32)).astype(BF)
                xs_b[o, :, part] = tail[d * rest : (d + 1) * rest].astype(BF)
                target = dev(e, lax.rem(xi + gx - d, gx), ci)
                for src, dst in [(xs_a, rx_a), (xs_b, rx_b)]:
                    send(src.at[o, :, part], dst.at[o, :, part], rx_r.at[2 * o + h], target)

    def to_column(k):
        for h in range(2):
            part = halves[h]
            sum_a = y0[k, 0:main, part] + rc[k, 0:main, part].astype(F32)
            tail = y0[k, side_main:, part] + rc[k, side_main:, part].astype(F32)
            sum_b = tail[0:rest]
            for d in range(1, gx):
                o = (d - 1) * experts + k
                count(cap * half_width, rx_r.at[2 * o + h])
                sum_a = sum_a + rx_a[o, :, part].astype(F32)
                sum_b = sum_b + rx_b[o, :, part].astype(F32)
            if k:
                zs_a[k, :, part] = sum_a.astype(BF)
                zs_b[k, :, part] = sum_b.astype(BF)
                target = dev(xor(e, k, experts), xi, ci)
                for src, dst in [(zs_a, z_a), (zs_b, z_b)]:
                    send(src.at[k, :, part], dst.at[k, :, part], rz_r.at[2 * k + h], target)
            else:
                z_all[0:main, part] = sum_a.astype(BF)
                z_stage[0:rest, part] = sum_b

    last = experts - 1
    from_column(0)
    from_chips(0)
    if last:
        from_column(1)
    for k in range(experts):
        first(k)
        if k:
            to_chips(k - 1)
            if k + 1 <= last:
                from_chips(k + 1)
        second(k)
        if k == 0:
            if last:
                from_chips(1)
            for relay in range(2, experts):
                from_column(relay)
    to_chips(last)
    for k in range(experts):
        to_column(k)

    early[3].wait()
    probs = lax.dot_general(
        normed, router[0], (((1,), (1,)), ((), ())), preferred_element_type=F32
    )
    probs = jnp.exp(probs - jnp.max(probs, axis=-1, keepdims=True))
    probs = probs / jnp.sum(probs, axis=-1, keepdims=True)
    prob_first = jnp.sum(probs * first_hot, axis=-1, keepdims=True)
    prob_second = jnp.sum(probs * second_hot, axis=-1, keepdims=True)
    gate = (prob_first * first_hot + prob_second * second_hot) / (prob_first + prob_second)
    combine = jnp.zeros((tok, lanes), F32)
    for k in range(experts):
        combine = combine + jnp.where(expert_of == k, gate[:, k : k + 1], 0.0)
    combine = (combine * placing)[:, 0:n_slots]
    high = combine.astype(BF)
    low = (combine - high.astype(F32)).astype(BF)

    early[4].wait()
    learner_in = student[0]
    shifted = learner_in - jnp.max(learner_in, axis=-1, keepdims=True)
    learner = shifted - jnp.log(jnp.sum(jnp.exp(shifted), axis=-1, keepdims=True))
    target_col = column(targets[0:1, :])
    vocab = student.shape[2]
    picked = lax.broadcasted_iota(jnp.int32, (tok, vocab), 1).astype(F32) == target_col
    hit = jnp.sum(jnp.where(picked, learner, 0.0), axis=-1, keepdims=True)
    loads[2].wait()

    for h in range(2):
        part = halves[h]
        for k in hop_order:
            count(cap * half_width, rz_r.at[2 * k + h])
            z_all[k * main : (k + 1) * main, part] = z_a[k, :, part]
            z_stage[k * rest : (k + 1) * rest, part] = z_b[k, :, part].astype(F32)
        z_all[n_main:, part] = z_stage[:, part].astype(BF)
        back = z_all[:, part]
        moe = jnp.dot(high, back, preferred_element_type=F32) + jnp.dot(
            low, back, preferred_element_type=F32
        )
        out_stage[:, part] = (mid[:, part] + moe).astype(BF)
    out = out_stage[...]
    out_copy = pltpu.make_async_copy(out_stage, layer_out.at[0], wsem.at[8])
    out_copy.start()

    final = layer_norm(out.astype(F32), gains[2]).astype(BF)
    logits = jnp.dot(final, short[...], preferred_element_type=F32)
    logits = logits - jnp.max(logits, axis=-1, keepdims=True)
    teacher = logits - jnp.log(jnp.sum(jnp.exp(logits), axis=-1, keepdims=True))
    token_loss = jnp.sum(jnp.exp(teacher) * (teacher - learner), axis=-1, keepdims=True) - hit
    counted = jnp.where(is_decoder, valid, 0.0)
    loss_sum = jnp.sum(token_loss * counted, axis=0, keepdims=True)
    loss_count = jnp.sum(counted, axis=0, keepdims=True)
    spot = lax.broadcasted_iota(jnp.int32, lsend.shape, 1)
    pair = jnp.where(spot == 0, loss_sum, jnp.where(spot == 1, loss_count, 0.0))
    lsend[...] = pair

    mine = (seg - half_seg) * n_exp + me
    n_loss = (n_seg - half_seg) * n_exp

    @pl.when(is_decoder)
    def _():
        lrecv[mine] = pair
        for ds in range(n_seg):
            for d in range(n_exp):
                if ds or d:
                    pltpu.make_async_remote_copy(
                        lsend, lrecv.at[mine], l_s, l_r,
                        device_id=peer(ds, d), device_id_type=MESH,
                    ).start()
        landed(lrecv.at[0 : n_loss - 1], l_r)

    @pl.when(seg < half_seg)
    def _():
        landed(lrecv, l_r)

    total = lrecv[0]
    for i in range(1, (n_seg - half_seg) * n_exp):
        total = total + lrecv[i]
    loss_out[...] = total[0:1, 0:1] / total[0:1, 1:2]

    @pl.when(is_decoder)
    def _():
        landed(lwide.at[0 : n_seg * n_exp - 1], l_s)

    out_copy.wait()
    moved = 2 * cap * (experts - 1 + (2 * gx - 1) * experts)
    left = moved * width // units
    while left:
        step = min(left, win.shape[0])
        landed(win.at[0:step], sent)
        left -= step

    @pl.when(seg < half_seg)
    def _():
        landed(kmem, msem.at[2])
        len_copy.wait_send()


def local(
    hidden, memory, lengths, memory_lengths, routes, norm_gain, router,
    w_in, w_out, shortlist, student, targets,
):
    n_seg = lax.axis_size("segment")
    n_exp = lax.axis_size("expert")
    experts = router.shape[2]
    group = n_exp // experts
    gc = 2
    gx = group // gc
    tok, width = hidden.shape[1], hidden.shape[2]
    units = w_in.shape[2]
    vocab = shortlist.shape[2]
    cap = 5 * tok // 8
    main = cap // 16 * 16
    rest = cap - main
    blocks = gx * experts
    vm = pl.BlockSpec(memory_space=pltpu.VMEM)
    hbm = pl.BlockSpec(memory_space=pl.ANY)
    v = pltpu.VMEM
    dma = pltpu.SemaphoreType.DMA
    nx = max(gx - 1, 1) * experts
    scratch = [
        v((1, tok, width), BF), v((1, 2, tok), jnp.int32), v((3, 1, width), F32),
        v((1, experts, width), BF), v((1, tok, vocab), F32), v((tok, width), BF),
        v((width, units), BF), v((units, width), BF), v((width, vocab), BF),
        v((tok, width), BF), v((8, 128), jnp.int32), v((8, 128), jnp.int32), v((tok, width), F32),
        v((experts, main, width), BF), v((experts, rest, width), BF),
        v((experts * gc * gx * cap, width), BF), v((gc * blocks, rest, width), BF),
        v((gx * rest, width), F32), v((gc * gx * cap, units), BF),
        v((experts, gx * cap, width), F32),
        v((experts, gx * cap, width), BF), v((experts, gx * cap, width), BF),
        v((nx, main, width), BF), v((nx, rest, width), BF),
        v((nx, main, width), BF), v((nx, rest, width), BF),
        v((experts, main, width), BF), v((experts, rest, width), BF),
        v((experts, main, width), BF), v((experts, rest, width), BF),
        v((experts * cap, width), BF), v((experts * rest, width), F32),
        v((1, 128), F32), v(((n_seg - n_seg // 2) * n_exp, 1, 128), F32),
        v((n_seg * n_exp, 1, 128), F32), v((cap * width // 1024, 8, 128), BF),
        dma((9,)), dma((7,)), dma((2 * blocks,)), dma((blocks,)),
        dma((2 * experts,)), dma((2 * nx,)), dma((2 * experts,)),
        dma(()), dma(()), dma(()),
    ]
    layer_out, loss = pl.pallas_call(
        functools.partial(kernel, n_seg, n_exp, experts, gx, gc),
        out_shape=(
            jax.ShapeDtypeStruct((1, tok, width), BF),
            jax.ShapeDtypeStruct((1, 1), F32),
        ),
        in_specs=[hbm, hbm, vm, vm, hbm, hbm, hbm, hbm, hbm, hbm, hbm, vm],
        out_specs=(hbm, vm),
        scratch_shapes=scratch,
        compiler_params=pltpu.CompilerParams(
            collective_id=0, has_side_effects=True, vmem_limit_bytes=60 * 1024 * 1024
        ),
    )(
        hidden, memory, lengths, memory_lengths, jnp.swapaxes(routes, 1, 2),
        jnp.swapaxes(norm_gain, 0, 1), jnp.swapaxes(router, 1, 2),
        w_in, w_out, shortlist, student, targets,
    )
    return layer_out, loss[0, 0]


def solution(mesh):
    placed = (
        P("segment", "expert", None),
        P("segment", "expert", None),
        P("segment", "expert"),
        P("segment", "expert"),
        P("segment", "expert", None),
        P("segment", None, None),
        P("segment", None, None),
        P("segment", None, "expert"),
        P("segment", "expert", None),
        P("segment", None, None),
        P("segment", "expert", None),
        P("segment", "expert"),
    )
    return jax.shard_map(
        local,
        mesh=mesh,
        in_specs=placed,
        out_specs=(P("segment", "expert", None), P()),
        check_vma=False,
    )
```

```python
import functools
import math

import jax
import jax.numpy as jnp
from jax import lax
from jax.experimental import pallas as pl
from jax.experimental.pallas import tpu as pltpu
from jax.sharding import PartitionSpec as P

HEAD_DIM = 128
LEN = 32
EPS = 1e-05
MESH = pl.DeviceIdType.MESH
BF = jnp.bfloat16
F32 = jnp.float32


def layer_norm(values, gain_row):
    centred = values - jnp.mean(values, axis=-1, keepdims=True)
    spread = jnp.mean(centred * centred, axis=-1, keepdims=True)
    return centred * lax.rsqrt(spread + EPS) * gain_row


def xor(a, k, count):
    out = 0
    bit = 1
    while bit < count:
        out = out + lax.rem(a // bit + (k // bit) % 2, 2) * bit
        bit *= 2
    return out


def kernel(
    n_seg, n_exp, experts, gx, gc,
    hidden_any, memory, lengths, memory_lengths, routes_any, gain_any, router_any,
    w_in, w_out, shortlist, student_any, targets,
    layer_out, loss_out,
    hidden, routes, norm_gain, router, student, out_stage,
    win, wout, short, kmem, klen_src, klen, mid,
    out_a, out_b, x, x_b, stage, act, y0,
    core, rc, xs_a, xs_b, rx_a, rx_b, zs_a, zs_b, z_a, z_b, z_all, z_stage,
    lsend, lrecv, lwide, tally,
    wsem, msem, ra, rb, rc_r, rx_r, rz_r, sent, l_s, l_r, met,
):
    seg = lax.axis_index("segment")
    me = lax.axis_index("expert")
    half_seg = n_seg // 2
    group = gx * gc
    e = me // group
    j = lax.rem(me, group)
    xi = j // gc
    ci = lax.rem(j, gc)
    tok = hidden.shape[1]
    width = hidden.shape[2]
    heads = width // HEAD_DIM
    cap = 5 * tok // 8
    main = cap // 16 * 16
    rest = cap - main
    hop_order = list(range(1, experts))

    def peer(ds, d):
        return (lax.rem(seg + ds, n_seg), lax.rem(me + d, n_exp))

    def dev(e2, x2, c2):
        return (seg, (e2 * gx + x2) * gc + c2)

    barrier = pltpu.get_barrier_semaphore()
    to_seg = lax.rem(seg + half_seg, n_seg)
    sides = [((e > 0), (lax.rem(e + experts - 1, experts))), ((e < experts - 1), lax.rem(e + 1, experts))]
    beside = (e > 0).astype(jnp.int32) + (e < experts - 1).astype(jnp.int32)

    def greet(sem):
        for there, e2 in sides:
            @pl.when(there)
            def _():
                pl.semaphore_signal(sem, inc=1, device_id=dev(e2, xi, ci), device_id_type=MESH)

    near = [(to_seg, me)]
    near += [dev(e, lax.rem(xi + d, gx), ci) for d in range(1, gx)]
    near += [dev(e, xi, lax.rem(ci + d, gc)) for d in range(1, gc)]
    for device in near:
        pl.semaphore_signal(barrier, inc=1, device_id=device, device_id_type=MESH)
    greet(barrier)

    early = [
        pltpu.make_async_copy(hidden_any, hidden, wsem.at[3]),
        pltpu.make_async_copy(gain_any, norm_gain, wsem.at[4]),
        pltpu.make_async_copy(routes_any, routes, wsem.at[5]),
        pltpu.make_async_copy(router_any, router, wsem.at[6]),
        pltpu.make_async_copy(student_any, student, wsem.at[7]),
    ]
    for load in early:
        load.start()
    loads = [
        pltpu.make_async_copy(w_in.at[0], win, wsem.at[0]),
        pltpu.make_async_copy(w_out.at[0], wout, wsem.at[1]),
        pltpu.make_async_copy(shortlist.at[0], short, wsem.at[2]),
    ]
    for load in loads:
        load.start()

    klen_src[...] = jnp.broadcast_to(memory_lengths[0:1, 0:1], klen_src.shape)
    for q in range(1, tok // LEN):
        klen_src[q : q + 1, :] = jnp.broadcast_to(memory_lengths[0:1, q : q + 1], (1, 128))
    pl.semaphore_wait(barrier, len(near) + beside)

    is_decoder = seg >= half_seg
    groups = 4
    band = width // groups
    mem_copies = [
        pltpu.make_async_remote_copy(
            memory.at[0, :, g * band : (g + 1) * band], kmem.at[:, g * band : (g + 1) * band],
            msem.at[2], msem.at[3 + g], device_id=(to_seg, me), device_id_type=MESH,
        )
        for g in range(groups)
    ]
    len_copy = pltpu.make_async_remote_copy(
        klen_src, klen, msem.at[0], msem.at[1], device_id=(to_seg, me), device_id_type=MESH
    )

    @pl.when(seg < half_seg)
    def _():
        len_copy.start()
        for copy in mem_copies:
            copy.start()

    rounds = max(experts - 2, 0)
    if rounds:
        greet(met.at[0])
    early[0].wait()
    early[1].wait()
    gains = [norm_gain[i] for i in range(3)]
    states = hidden[0].astype(F32)

    @pl.when(seg < half_seg)
    def _():
        mid[...] = states

    @pl.when(seg >= half_seg)
    def _():
        queries = layer_norm(states, gains[0]).astype(BF)
        len_copy.wait_recv()
        col = lax.broadcasted_iota(jnp.int32, (tok, tok), 1)
        row = lax.broadcasted_iota(jnp.int32, (tok, tok), 0)
        klen_v = klen[...]
        allowed = jnp.zeros((tok, tok), jnp.bool_)
        for q in range(tok // LEN):
            inside = (col >= q * LEN) & (col - q * LEN < klen_v[q : q + 1, 0:1])
            inside = inside & (col < (q + 1) * LEN) & (row >= q * LEN) & (row < (q + 1) * LEN)
            allowed = allowed | inside
        for g in range(groups):
            mem_copies[g].wait_recv()
            keys = kmem[:, g * band : (g + 1) * band]
            parts = [slice(h * HEAD_DIM, (h + 1) * HEAD_DIM) for h in range(band // HEAD_DIM)]
            scores = jnp.concatenate(
                [
                    jnp.where(
                        allowed,
                        lax.dot_general(
                            queries[:, g * band + part.start : g * band + part.stop], keys[:, part],
                            (((1,), (1,)), ((), ())), preferred_element_type=F32,
                        )
                        * (1.0 / math.sqrt(HEAD_DIM)),
                        -1e30,
                    )
                    for part in parts
                ],
                axis=0,
            )
            top = jnp.max(scores, axis=-1, keepdims=True)
            raised = jnp.exp(scores - top)
            weights = (raised / jnp.sum(raised, axis=-1, keepdims=True)).astype(BF)
            for h, part in enumerate(parts):
                here = slice(g * band + part.start, g * band + part.stop)
                mid[:, here] = states[:, here] + jnp.dot(
                    weights[h * tok : (h + 1) * tok], keys[:, part], preferred_element_type=F32
                )

    for i in range(rounds):
        pl.semaphore_wait(met.at[i], beside)
        if i + 1 < rounds:
            greet(met.at[i + 1])

    normed = layer_norm(mid[...], gains[1]).astype(BF)

    early[2].wait()
    expert_lane = lax.broadcasted_iota(jnp.int32, (tok, experts), 1)
    pos = lax.broadcasted_iota(jnp.int32, (tok, 1), 0)
    valid = jnp.zeros((tok, 1), F32)
    for q in range(tok // LEN):
        ok = (pos >= q * LEN) & (pos < (q + 1) * LEN) & (pos - q * LEN < lengths[0:1, q : q + 1])
        valid = valid + ok.astype(F32)
    square = lax.broadcasted_iota(jnp.int32, (tok, tok), 0) == lax.broadcasted_iota(
        jnp.int32, (tok, tok), 1
    )

    def column(row):
        spread = jnp.where(square, jnp.broadcast_to(row, (tok, tok)), 0)
        return jnp.sum(spread.astype(F32), axis=-1, keepdims=True)

    expert_lane = expert_lane.astype(F32)
    first_hot = (column(routes[0, 0:1, :]) == expert_lane).astype(F32)
    second_hot = (column(routes[0, 1:2, :]) == expert_lane).astype(F32)
    chosen = (first_hot + second_hot) * valid
    before = (
        lax.broadcasted_iota(jnp.int32, (tok, tok), 1)
        < lax.broadcasted_iota(jnp.int32, (tok, tok), 0)
    ).astype(BF)
    rank = jnp.dot(before, chosen.astype(BF), preferred_element_type=F32)
    n_main = experts * main
    n_slots = experts * cap
    lanes = -(-n_slots // 128) * 128
    lane = lax.broadcasted_iota(jnp.int32, (1, lanes), 1)
    slot_of = jnp.full((1, lanes), -1, jnp.int32)
    expert_of = jnp.full((1, lanes), -1, jnp.int32)
    for k in range(experts):
        ek = xor(e, k, experts)
        in_main = (lane >= k * main) & (lane < (k + 1) * main)
        low = n_main + k * rest
        in_rest = (lane >= low) & (lane < low + rest)
        slot_of = jnp.where(in_main, lane - k * main, slot_of)
        slot_of = jnp.where(in_rest, lane - low + main, slot_of)
        expert_of = jnp.where(in_main | in_rest, ek, expert_of)
    placing = jnp.zeros((tok, lanes), F32)
    for k in range(experts):
        here = (expert_of == k) & (rank[:, k : k + 1] == slot_of.astype(F32))
        placing = placing + jnp.where(here, chosen[:, k : k + 1], 0.0)
    place_rows = jnp.transpose(placing)[0:n_slots].astype(BF)
    slots = jnp.dot(place_rows, normed, preferred_element_type=F32)

    chunk = gc * gx * cap
    side = gx * cap
    side_main = gx * main
    half_width = width // 2
    halves = [slice(h * half_width, (h + 1) * half_width) for h in range(2)]

    def rows_a(dc, dx, k):
        return pl.ds(k * chunk + dc * side + dx * main, main)

    def index_b(dc, dx, k):
        return (dc * gx + dx) * experts + k

    for k in hop_order:
        out_a[k] = slots[k * main : (k + 1) * main].astype(BF)
        out_b[k] = slots[n_main + k * rest : n_main + (k + 1) * rest].astype(BF)
    x[rows_a(0, 0, 0), :] = slots[0:main].astype(BF)
    x_b[0] = slots[n_main : n_main + rest].astype(BF)

    def send(src, dst, r_sem, target):
        pltpu.make_async_remote_copy(
            src, dst, sent, r_sem, device_id=target, device_id_type=MESH
        ).start()

    def landed(ref, sem):
        pltpu.make_async_copy(ref, ref, sem).wait()

    def count(size, sem):
        landed(tally.at[0 : size // 1024], sem)

    def piece(slot, p):
        if p < 2:
            return x.at[rows_a(*slot), halves[p]]
        return x_b.at[index_b(*slot)]

    def mark(slot, p):
        if slot[0]:
            return rb.at[slot[1] * experts + slot[2]]
        return ra.at[2 * (slot[1] * experts + slot[2]) + min(p, 1)]

    def arrived(slot, p):
        if p == 0:
            landed(piece(slot, 0), mark(slot, 0))
        elif p == 1:
            count(main * half_width + rest * width, mark(slot, 1))

    def forward(slot_from, slot_to, p, target):
        send(piece(slot_from, p), piece(slot_to, p), mark(slot_to, p), target)

    for k in hop_order:
        target = dev(xor(e, k, experts), xi, ci)
        for p in range(3):
            src = out_a.at[k, :, halves[p]] if p < 2 else out_b.at[k]
            send(src, piece((0, 0, k), p), mark((0, 0, k), p), target)

    core_dev = dev(e, xi, lax.rem(ci + 1, gc))

    def from_column(k):
        for p in range(3):
            if k:
                arrived((0, 0, k), p)
            for d in range(1, gx):
                forward((0, 0, k), (0, d, k), p, dev(e, lax.rem(xi + d, gx), ci))
            forward((0, 0, k), (1, 0, k), p, core_dev)

    def from_chips(k):
        for p in range(3):
            for d in range(1, gx):
                arrived((0, d, k), p)
                forward((0, d, k), (1, d, k), p, core_dev)

    units = win.shape[1]
    tile = min(1024, units)
    tile2 = min(1024, half_width)

    def first(k):
        for d in range(gx):
            count(cap * width, mark((1, d, k), 0))
        for dc in range(gc):
            for d in range(gx):
                stage[d * rest : (d + 1) * rest, :] = x_b[index_b(dc, d, k)].astype(F32)
            low = k * chunk + dc * side + side_main
            x[low : low + gx * rest, :] = stage[...].astype(BF)
        if k == 0:
            loads[0].wait()
        rows = slice(k * chunk, (k + 1) * chunk)

        @pl.loop(0, units // tile)
        def _(i):
            cols = pl.ds(pl.multiple_of(i * tile, tile), tile)
            act[:, cols] = jnp.maximum(
                jnp.dot(x[rows, :], win[:, cols], preferred_element_type=F32), 0.0
            ).astype(BF)

    def second(k):
        if k == 0:
            loads[1].wait()
        for h in range(2):
            @pl.loop(0, half_width // tile2)
            def _(i):
                cols = pl.ds(pl.multiple_of(h * half_width + i * tile2, tile2), tile2)
                part = jnp.dot(act[...], wout[:, cols], preferred_element_type=F32)
                core[k, :, cols] = part[side:].astype(BF)
                y0[k, :, cols] = part[0:side]

            send(core.at[k, :, halves[h]], rc.at[k, :, halves[h]], rc_r.at[2 * k + h], core_dev)

    def to_chips(k):
        for h in range(2):
            part = halves[h]
            landed(rc.at[k, :, part], rc_r.at[2 * k + h])
            tail = y0[k, side_main:, part] + rc[k, side_main:, part].astype(F32)
            for d in range(1, gx):
                o = (d - 1) * experts + k
                rows = slice(d * main, (d + 1) * main)
                xs_a[o, :, part] = (y0[k, rows, part] + rc[k, rows, part].astype(F32)).astype(BF)
                xs_b[o, :, part] = tail[d * rest : (d + 1) * rest].astype(BF)
                target = dev(e, lax.rem(xi + gx - d, gx), ci)
                for src, dst in [(xs_a, rx_a), (xs_b, rx_b)]:
                    send(src.at[o, :, part], dst.at[o, :, part], rx_r.at[2 * o + h], target)

    def to_column(k):
        for h in range(2):
            part = halves[h]
            sum_a = y0[k, 0:main, part] + rc[k, 0:main, part].astype(F32)
            tail = y0[k, side_main:, part] + rc[k, side_main:, part].astype(F32)
            sum_b = tail[0:rest]
            for d in range(1, gx):
                o = (d - 1) * experts + k
                count(cap * half_width, rx_r.at[2 * o + h])
                sum_a = sum_a + rx_a[o, :, part].astype(F32)
                sum_b = sum_b + rx_b[o, :, part].astype(F32)
            if k:
                zs_a[k, :, part] = sum_a.astype(BF)
                zs_b[k, :, part] = sum_b.astype(BF)
                target = dev(xor(e, k, experts), xi, ci)
                for src, dst in [(zs_a, z_a), (zs_b, z_b)]:
                    send(src.at[k, :, part], dst.at[k, :, part], rz_r.at[2 * k + h], target)
            else:
                z_all[0:main, part] = sum_a.astype(BF)
                z_stage[0:rest, part] = sum_b

    last = experts - 1
    from_column(0)
    from_chips(0)
    if last:
        from_column(1)
    for k in range(experts):
        first(k)
        if k:
            to_chips(k - 1)
        if k > 1 and k + 1 <= last:
            from_chips(k + 1)
        second(k)
        if k == 1 and k + 1 <= last:
            from_chips(k + 1)
        if k == 0:
            if last:
                from_chips(1)
            for relay in range(2, experts):
                from_column(relay)
    to_chips(last)
    for k in range(experts):
        to_column(k)

    early[3].wait()
    probs = lax.dot_general(
        normed, router[0], (((1,), (1,)), ((), ())), preferred_element_type=F32
    )
    probs = jnp.exp(probs - jnp.max(probs, axis=-1, keepdims=True))
    probs = probs / jnp.sum(probs, axis=-1, keepdims=True)
    prob_first = jnp.sum(probs * first_hot, axis=-1, keepdims=True)
    prob_second = jnp.sum(probs * second_hot, axis=-1, keepdims=True)
    gate = (prob_first * first_hot + prob_second * second_hot) / (prob_first + prob_second)
    combine = jnp.zeros((tok, lanes), F32)
    for k in range(experts):
        combine = combine + jnp.where(expert_of == k, gate[:, k : k + 1], 0.0)
    combine = (combine * placing)[:, 0:n_slots]
    high = combine.astype(BF)
    low = (combine - high.astype(F32)).astype(BF)

    early[4].wait()
    learner_in = student[0]
    shifted = learner_in - jnp.max(learner_in, axis=-1, keepdims=True)
    learner = shifted - jnp.log(jnp.sum(jnp.exp(shifted), axis=-1, keepdims=True))
    target_col = column(targets[0:1, :])
    vocab = student.shape[2]
    picked = lax.broadcasted_iota(jnp.int32, (tok, vocab), 1).astype(F32) == target_col
    hit = jnp.sum(jnp.where(picked, learner, 0.0), axis=-1, keepdims=True)
    loads[2].wait()

    for h in range(2):
        part = halves[h]
        for k in hop_order:
            count(cap * half_width, rz_r.at[2 * k + h])
            z_all[k * main : (k + 1) * main, part] = z_a[k, :, part]
            z_stage[k * rest : (k + 1) * rest, part] = z_b[k, :, part].astype(F32)
        z_all[n_main:, part] = z_stage[:, part].astype(BF)
        back = z_all[:, part]
        moe = jnp.dot(high, back, preferred_element_type=F32) + jnp.dot(
            low, back, preferred_element_type=F32
        )
        out_stage[:, part] = (mid[:, part] + moe).astype(BF)
    out = out_stage[...]
    out_copy = pltpu.make_async_copy(out_stage, layer_out.at[0], wsem.at[8])
    out_copy.start()

    final = layer_norm(out.astype(F32), gains[2]).astype(BF)
    logits = jnp.dot(final, short[...], preferred_element_type=F32)
    logits = logits - jnp.max(logits, axis=-1, keepdims=True)
    teacher = logits - jnp.log(jnp.sum(jnp.exp(logits), axis=-1, keepdims=True))
    token_loss = jnp.sum(jnp.exp(teacher) * (teacher - learner), axis=-1, keepdims=True) - hit
    counted = jnp.where(is_decoder, valid, 0.0)
    loss_sum = jnp.sum(token_loss * counted, axis=0, keepdims=True)
    loss_count = jnp.sum(counted, axis=0, keepdims=True)
    spot = lax.broadcasted_iota(jnp.int32, lsend.shape, 1)
    pair = jnp.where(spot == 0, loss_sum, jnp.where(spot == 1, loss_count, 0.0))
    lsend[...] = pair

    mine = (seg - half_seg) * n_exp + me
    n_loss = (n_seg - half_seg) * n_exp

    @pl.when(is_decoder)
    def _():
        lrecv[mine] = pair
        for ds in range(n_seg):
            for d in range(n_exp):
                if ds or d:
                    pltpu.make_async_remote_copy(
                        lsend, lrecv.at[mine], l_s, l_r,
                        device_id=peer(ds, d), device_id_type=MESH,
                    ).start()
        landed(lrecv.at[0 : n_loss - 1], l_r)

    @pl.when(seg < half_seg)
    def _():
        landed(lrecv, l_r)

    total = lrecv[0]
    for i in range(1, (n_seg - half_seg) * n_exp):
        total = total + lrecv[i]
    loss_out[...] = total[0:1, 0:1] / total[0:1, 1:2]

    @pl.when(is_decoder)
    def _():
        landed(lwide.at[0 : n_seg * n_exp - 1], l_s)

    out_copy.wait()
    moved = 2 * cap * (experts - 1 + (2 * gx - 1) * experts)
    left = moved * width // units
    while left:
        step = min(left, win.shape[0])
        landed(win.at[0:step], sent)
        left -= step

    @pl.when(seg < half_seg)
    def _():
        landed(kmem, msem.at[2])
        len_copy.wait_send()


def local(
    hidden, memory, lengths, memory_lengths, routes, norm_gain, router,
    w_in, w_out, shortlist, student, targets,
):
    n_seg = lax.axis_size("segment")
    n_exp = lax.axis_size("expert")
    experts = router.shape[2]
    group = n_exp // experts
    gc = 2
    gx = group // gc
    tok, width = hidden.shape[1], hidden.shape[2]
    units = w_in.shape[2]
    vocab = shortlist.shape[2]
    cap = 5 * tok // 8
    main = cap // 16 * 16
    rest = cap - main
    blocks = gx * experts
    vm = pl.BlockSpec(memory_space=pltpu.VMEM)
    hbm = pl.BlockSpec(memory_space=pl.ANY)
    v = pltpu.VMEM
    dma = pltpu.SemaphoreType.DMA
    nx = max(gx - 1, 1) * experts
    scratch = [
        v((1, tok, width), BF), v((1, 2, tok), jnp.int32), v((3, 1, width), F32),
        v((1, experts, width), BF), v((1, tok, vocab), F32), v((tok, width), BF),
        v((width, units), BF), v((units, width), BF), v((width, vocab), BF),
        v((tok, width), BF), v((8, 128), jnp.int32), v((8, 128), jnp.int32), v((tok, width), F32),
        v((experts, main, width), BF), v((experts, rest, width), BF),
        v((experts * gc * gx * cap, width), BF), v((gc * blocks, rest, width), BF),
        v((gx * rest, width), F32), v((gc * gx * cap, units), BF),
        v((experts, gx * cap, width), F32),
        v((experts, gx * cap, width), BF), v((experts, gx * cap, width), BF),
        v((nx, main, width), BF), v((nx, rest, width), BF),
        v((nx, main, width), BF), v((nx, rest, width), BF),
        v((experts, main, width), BF), v((experts, rest, width), BF),
        v((experts, main, width), BF), v((experts, rest, width), BF),
        v((experts * cap, width), BF), v((experts * rest, width), F32),
        v((1, 128), F32), v(((n_seg - n_seg // 2) * n_exp, 1, 128), F32),
        v((n_seg * n_exp, 1, 128), F32), v((cap * width // 1024, 8, 128), BF),
        dma((9,)), dma((7,)), dma((2 * blocks,)), dma((blocks,)),
        dma((2 * experts,)), dma((2 * nx,)), dma((2 * experts,)),
        dma(()), dma(()), dma(()), pltpu.SemaphoreType.REGULAR((max(experts - 2, 1),)),
    ]
    layer_out, loss = pl.pallas_call(
        functools.partial(kernel, n_seg, n_exp, experts, gx, gc),
        out_shape=(
            jax.ShapeDtypeStruct((1, tok, width), BF),
            jax.ShapeDtypeStruct((1, 1), F32),
        ),
        in_specs=[hbm, hbm, vm, vm, hbm, hbm, hbm, hbm, hbm, hbm, hbm, vm],
        out_specs=(hbm, vm),
        scratch_shapes=scratch,
        compiler_params=pltpu.CompilerParams(
            collective_id=0, has_side_effects=True, vmem_limit_bytes=60 * 1024 * 1024
        ),
    )(
        hidden, memory, lengths, memory_lengths, jnp.swapaxes(routes, 1, 2),
        jnp.swapaxes(norm_gain, 0, 1), jnp.swapaxes(router, 1, 2),
        w_in, w_out, shortlist, student, targets,
    )
    return layer_out, loss[0, 0]


def solution(mesh):
    placed = (
        P("segment", "expert", None),
        P("segment", "expert", None),
        P("segment", "expert"),
        P("segment", "expert"),
        P("segment", "expert", None),
        P("segment", None, None),
        P("segment", None, None),
        P("segment", None, "expert"),
        P("segment", "expert", None),
        P("segment", None, None),
        P("segment", "expert", None),
        P("segment", "expert"),
    )
    return jax.shard_map(
        local,
        mesh=mesh,
        in_specs=placed,
        out_specs=(P("segment", "expert", None), P()),
        check_vma=False,
    )
```

```python
import functools
import math

import jax
import jax.numpy as jnp
from jax import lax
from jax.experimental import pallas as pl
from jax.experimental.pallas import tpu as pltpu
from jax.sharding import PartitionSpec as P

HEAD_DIM = 128
LEN = 32
EPS = 1e-05
MESH = pl.DeviceIdType.MESH
BF = jnp.bfloat16
F32 = jnp.float32


def layer_norm(values, gain_row):
    centred = values - jnp.mean(values, axis=-1, keepdims=True)
    spread = jnp.mean(centred * centred, axis=-1, keepdims=True)
    return centred * lax.rsqrt(spread + EPS) * gain_row


def xor(a, k, count):
    out = 0
    bit = 1
    while bit < count:
        out = out + lax.rem(a // bit + (k // bit) % 2, 2) * bit
        bit *= 2
    return out


def kernel(
    n_seg, n_exp, experts, gx, gc,
    hidden_any, memory, lengths, memory_lengths, routes_any, gain_any, router_any,
    w_in, w_out, shortlist, student_any, targets,
    layer_out, loss_out,
    hidden, routes, norm_gain, router, student, out_stage,
    win, wout, short, kmem, klen_src, klen, mid,
    out_a, out_b, x, x_b, stage, act, y0,
    core, rc, xs_a, xs_b, rx_a, rx_b, zs_a, zs_b, z_a, z_b, z_all, z_stage,
    lsend, lrecv, lwide, tally,
    wsem, msem, ra, rb, rc_r, rx_r, rz_r, sent, l_s, l_r, met,
):
    seg = lax.axis_index("segment")
    me = lax.axis_index("expert")
    half_seg = n_seg // 2
    group = gx * gc
    e = me // group
    j = lax.rem(me, group)
    xi = j // gc
    ci = lax.rem(j, gc)
    tok = hidden.shape[1]
    width = hidden.shape[2]
    heads = width // HEAD_DIM
    cap = 5 * tok // 8
    main = cap // 16 * 16
    rest = cap - main
    hop_order = list(range(1, experts))

    def peer(ds, d):
        return (lax.rem(seg + ds, n_seg), lax.rem(me + d, n_exp))

    def dev(e2, x2, c2):
        return (seg, (e2 * gx + x2) * gc + c2)

    barrier = pltpu.get_barrier_semaphore()
    to_seg = lax.rem(seg + half_seg, n_seg)
    sides = [((e > 0), (lax.rem(e + experts - 1, experts))), ((e < experts - 1), lax.rem(e + 1, experts))]
    beside = (e > 0).astype(jnp.int32) + (e < experts - 1).astype(jnp.int32)

    def greet(sem):
        for there, e2 in sides:
            @pl.when(there)
            def _():
                pl.semaphore_signal(sem, inc=1, device_id=dev(e2, xi, ci), device_id_type=MESH)

    near = [(to_seg, me)]
    near += [dev(e, lax.rem(xi + d, gx), ci) for d in range(1, gx)]
    near += [dev(e, xi, lax.rem(ci + d, gc)) for d in range(1, gc)]
    for device in near:
        pl.semaphore_signal(barrier, inc=1, device_id=device, device_id_type=MESH)
    greet(barrier)

    early = [
        pltpu.make_async_copy(hidden_any, hidden, wsem.at[3]),
        pltpu.make_async_copy(gain_any, norm_gain, wsem.at[4]),
        pltpu.make_async_copy(routes_any, routes, wsem.at[5]),
        pltpu.make_async_copy(router_any, router, wsem.at[6]),
        pltpu.make_async_copy(student_any, student, wsem.at[7]),
    ]
    for load in early:
        load.start()
    loads = [
        pltpu.make_async_copy(w_in.at[0], win, wsem.at[0]),
        pltpu.make_async_copy(w_out.at[0], wout, wsem.at[1]),
        pltpu.make_async_copy(shortlist.at[0], short, wsem.at[2]),
    ]
    klen_src[...] = jnp.broadcast_to(memory_lengths[0:1, 0:1], klen_src.shape)
    for q in range(1, tok // LEN):
        klen_src[q : q + 1, :] = jnp.broadcast_to(memory_lengths[0:1, q : q + 1], (1, 128))
    pl.semaphore_wait(barrier, len(near) + beside)

    is_decoder = seg >= half_seg
    groups = 4
    band = width // groups
    mem_copies = [
        pltpu.make_async_remote_copy(
            memory.at[0, :, g * band : (g + 1) * band], kmem.at[:, g * band : (g + 1) * band],
            msem.at[2], msem.at[3 + g], device_id=(to_seg, me), device_id_type=MESH,
        )
        for g in range(groups)
    ]
    len_copy = pltpu.make_async_remote_copy(
        klen_src, klen, msem.at[0], msem.at[1], device_id=(to_seg, me), device_id_type=MESH
    )

    @pl.when(seg < half_seg)
    def _():
        len_copy.start()
        for copy in mem_copies:
            copy.start()

    for load in loads:
        load.start()

    rounds = max(experts - 2, 0)
    if rounds:
        greet(met.at[0])
    early[0].wait()
    early[1].wait()
    gains = [norm_gain[i] for i in range(3)]
    states = hidden[0].astype(F32)

    queries = layer_norm(states, gains[0]).astype(BF)
    for i in range(rounds - 1):
        pl.semaphore_wait(met.at[i], beside)
        greet(met.at[i + 1])

    early[2].wait()
    expert_lane = lax.broadcasted_iota(jnp.int32, (tok, experts), 1)
    pos = lax.broadcasted_iota(jnp.int32, (tok, 1), 0)
    valid = jnp.zeros((tok, 1), F32)
    for q in range(tok // LEN):
        ok = (pos >= q * LEN) & (pos < (q + 1) * LEN) & (pos - q * LEN < lengths[0:1, q : q + 1])
        valid = valid + ok.astype(F32)
    square = lax.broadcasted_iota(jnp.int32, (tok, tok), 0) == lax.broadcasted_iota(
        jnp.int32, (tok, tok), 1
    )

    def column(row):
        spread = jnp.where(square, jnp.broadcast_to(row, (tok, tok)), 0)
        return jnp.sum(spread.astype(F32), axis=-1, keepdims=True)

    expert_lane = expert_lane.astype(F32)
    first_hot = (column(routes[0, 0:1, :]) == expert_lane).astype(F32)
    second_hot = (column(routes[0, 1:2, :]) == expert_lane).astype(F32)
    chosen = (first_hot + second_hot) * valid
    before = (
        lax.broadcasted_iota(jnp.int32, (tok, tok), 1)
        < lax.broadcasted_iota(jnp.int32, (tok, tok), 0)
    ).astype(BF)
    rank = jnp.dot(before, chosen.astype(BF), preferred_element_type=F32)
    n_main = experts * main
    n_slots = experts * cap
    lanes = -(-n_slots // 128) * 128
    lane = lax.broadcasted_iota(jnp.int32, (1, lanes), 1)
    slot_of = jnp.full((1, lanes), -1, jnp.int32)
    expert_of = jnp.full((1, lanes), -1, jnp.int32)
    for k in range(experts):
        ek = xor(e, k, experts)
        in_main = (lane >= k * main) & (lane < (k + 1) * main)
        low = n_main + k * rest
        in_rest = (lane >= low) & (lane < low + rest)
        slot_of = jnp.where(in_main, lane - k * main, slot_of)
        slot_of = jnp.where(in_rest, lane - low + main, slot_of)
        expert_of = jnp.where(in_main | in_rest, ek, expert_of)
    placing = jnp.zeros((tok, lanes), F32)
    for k in range(experts):
        here = (expert_of == k) & (rank[:, k : k + 1] == slot_of.astype(F32))
        placing = placing + jnp.where(here, chosen[:, k : k + 1], 0.0)
    place_rows = jnp.transpose(placing)[0:n_slots].astype(BF)
    @pl.when(seg < half_seg)
    def _():
        mid[...] = states

    @pl.when(seg >= half_seg)
    def _():
        len_copy.wait_recv()
        col = lax.broadcasted_iota(jnp.int32, (tok, tok), 1)
        row = lax.broadcasted_iota(jnp.int32, (tok, tok), 0)
        klen_v = klen[...]
        allowed = jnp.zeros((tok, tok), jnp.bool_)
        for q in range(tok // LEN):
            inside = (col >= q * LEN) & (col - q * LEN < klen_v[q : q + 1, 0:1])
            inside = inside & (col < (q + 1) * LEN) & (row >= q * LEN) & (row < (q + 1) * LEN)
            allowed = allowed | inside
        for g in range(groups):
            mem_copies[g].wait_recv()
            keys = kmem[:, g * band : (g + 1) * band]
            parts = [slice(h * HEAD_DIM, (h + 1) * HEAD_DIM) for h in range(band // HEAD_DIM)]
            scores = jnp.concatenate(
                [
                    jnp.where(
                        allowed,
                        lax.dot_general(
                            queries[:, g * band + part.start : g * band + part.stop], keys[:, part],
                            (((1,), (1,)), ((), ())), preferred_element_type=F32,
                        )
                        * (1.0 / math.sqrt(HEAD_DIM)),
                        -1e30,
                    )
                    for part in parts
                ],
                axis=0,
            )
            top = jnp.max(scores, axis=-1, keepdims=True)
            raised = jnp.exp(scores - top)
            weights = (raised / jnp.sum(raised, axis=-1, keepdims=True)).astype(BF)
            for h, part in enumerate(parts):
                here = slice(g * band + part.start, g * band + part.stop)
                mid[:, here] = states[:, here] + jnp.dot(
                    weights[h * tok : (h + 1) * tok], keys[:, part], preferred_element_type=F32
                )

    if rounds:
        pl.semaphore_wait(met.at[rounds - 1], beside)

    normed = layer_norm(mid[...], gains[1]).astype(BF)

    slots = jnp.dot(place_rows, normed, preferred_element_type=F32)

    chunk = gc * gx * cap
    side = gx * cap
    side_main = gx * main
    half_width = width // 2
    halves = [slice(h * half_width, (h + 1) * half_width) for h in range(2)]

    def rows_a(dc, dx, k):
        return pl.ds(k * chunk + dc * side + dx * main, main)

    def index_b(dc, dx, k):
        return (dc * gx + dx) * experts + k

    for k in hop_order:
        out_a[k] = slots[k * main : (k + 1) * main].astype(BF)
        out_b[k] = slots[n_main + k * rest : n_main + (k + 1) * rest].astype(BF)
    x[rows_a(0, 0, 0), :] = slots[0:main].astype(BF)
    x_b[0] = slots[n_main : n_main + rest].astype(BF)

    def send(src, dst, r_sem, target):
        pltpu.make_async_remote_copy(
            src, dst, sent, r_sem, device_id=target, device_id_type=MESH
        ).start()

    def landed(ref, sem):
        pltpu.make_async_copy(ref, ref, sem).wait()

    def count(size, sem):
        landed(tally.at[0 : size // 1024], sem)

    def piece(slot, p):
        if p < 2:
            return x.at[rows_a(*slot), halves[p]]
        return x_b.at[index_b(*slot)]

    def mark(slot, p):
        if slot[0]:
            return rb.at[slot[1] * experts + slot[2]]
        return ra.at[2 * (slot[1] * experts + slot[2]) + min(p, 1)]

    def arrived(slot, p):
        if p == 0:
            landed(piece(slot, 0), mark(slot, 0))
        elif p == 1:
            count(main * half_width + rest * width, mark(slot, 1))

    def forward(slot_from, slot_to, p, target):
        send(piece(slot_from, p), piece(slot_to, p), mark(slot_to, p), target)

    for k in hop_order:
        target = dev(xor(e, k, experts), xi, ci)
        for p in range(3):
            src = out_a.at[k, :, halves[p]] if p < 2 else out_b.at[k]
            send(src, piece((0, 0, k), p), mark((0, 0, k), p), target)

    core_dev = dev(e, xi, lax.rem(ci + 1, gc))

    def from_column(k):
        for p in range(3):
            if k:
                arrived((0, 0, k), p)
            for d in range(1, gx):
                forward((0, 0, k), (0, d, k), p, dev(e, lax.rem(xi + d, gx), ci))
            forward((0, 0, k), (1, 0, k), p, core_dev)

    def from_chips(k):
        for p in range(3):
            for d in range(1, gx):
                arrived((0, d, k), p)
                forward((0, d, k), (1, d, k), p, core_dev)

    units = win.shape[1]
    tile = min(1024, units)
    tile2 = min(1024, half_width)

    def first(k):
        for d in range(gx):
            count(cap * width, mark((1, d, k), 0))
        for dc in range(gc):
            for d in range(gx):
                stage[d * rest : (d + 1) * rest, :] = x_b[index_b(dc, d, k)].astype(F32)
            low = k * chunk + dc * side + side_main
            x[low : low + gx * rest, :] = stage[...].astype(BF)
        if k == 0:
            loads[0].wait()
        rows = slice(k * chunk, (k + 1) * chunk)

        @pl.loop(0, units // tile)
        def _(i):
            cols = pl.ds(pl.multiple_of(i * tile, tile), tile)
            act[k, :, cols] = jnp.maximum(
                jnp.dot(x[rows, :], win[:, cols], preferred_element_type=F32), 0.0
            ).astype(BF)

    def second(k):
        if k == 0:
            loads[1].wait()
        for h in range(2):
            @pl.loop(0, half_width // tile2)
            def _(i):
                cols = pl.ds(pl.multiple_of(h * half_width + i * tile2, tile2), tile2)
                part = jnp.dot(act[k], wout[:, cols], preferred_element_type=F32)
                core[k, :, cols] = part[side:].astype(BF)
                y0[k, :, cols] = part[0:side]

            send(core.at[k, :, halves[h]], rc.at[k, :, halves[h]], rc_r.at[2 * k + h], core_dev)

    def to_chips(k):
        for h in range(2):
            part = halves[h]
            landed(rc.at[k, :, part], rc_r.at[2 * k + h])
            tail = y0[k, side_main:, part] + rc[k, side_main:, part].astype(F32)
            for d in range(1, gx):
                o = (d - 1) * experts + k
                rows = slice(d * main, (d + 1) * main)
                xs_a[o, :, part] = (y0[k, rows, part] + rc[k, rows, part].astype(F32)).astype(BF)
                xs_b[o, :, part] = tail[d * rest : (d + 1) * rest].astype(BF)
                target = dev(e, lax.rem(xi + gx - d, gx), ci)
                for src, dst in [(xs_a, rx_a), (xs_b, rx_b)]:
                    send(src.at[o, :, part], dst.at[o, :, part], rx_r.at[2 * o + h], target)

    def to_column(k):
        for h in range(2):
            part = halves[h]
            sum_a = y0[k, 0:main, part] + rc[k, 0:main, part].astype(F32)
            tail = y0[k, side_main:, part] + rc[k, side_main:, part].astype(F32)
            sum_b = tail[0:rest]
            for d in range(1, gx):
                o = (d - 1) * experts + k
                count(cap * half_width, rx_r.at[2 * o + h])
                sum_a = sum_a + rx_a[o, :, part].astype(F32)
                sum_b = sum_b + rx_b[o, :, part].astype(F32)
            if k:
                zs_a[k, :, part] = sum_a.astype(BF)
                zs_b[k, :, part] = sum_b.astype(BF)
                target = dev(xor(e, k, experts), xi, ci)
                for src, dst in [(zs_a, z_a), (zs_b, z_b)]:
                    send(src.at[k, :, part], dst.at[k, :, part], rz_r.at[2 * k + h], target)
            else:
                z_all[0:main, part] = sum_a.astype(BF)
                z_stage[0:rest, part] = sum_b

    last = experts - 1

    def relay(core_side, steps):
        steps = [(step, k) for step, k in steps if k <= last]
        if steps:
            @pl.when((ci > 0) if core_side else (ci == 0))
            def _():
                for step, k in steps:
                    step(k)

    far = range(2, experts)
    from_column(0)
    from_chips(0)
    if last:
        from_column(1)
    relay(1, [(from_column, 2)])
    first(0)
    relay(1, [(from_chips, 1), (from_column, 3)])
    second(0)
    relay(0, [(from_column, k) for k in far] + [(from_chips, 1)])
    relay(1, [(from_column, k) for k in far if k > 3] + [(from_chips, 2)])
    if last:
        first(1)
    to_chips(0)
    relay(0, [(from_chips, 2)])
    for k in far:
        relay(1, [(from_chips, k + 1)])
        first(k)
        relay(0, [(from_chips, k + 1)])
        if k > 2:
            to_chips(k - 1)
        second(k)
    if last:
        second(1)
    if last > 1:
        to_chips(last)
    if last:
        to_chips(1)
    for k in [*far, *range(min(experts, 2))]:
        to_column(k)

    early[3].wait()
    probs = lax.dot_general(
        normed, router[0], (((1,), (1,)), ((), ())), preferred_element_type=F32
    )
    probs = jnp.exp(probs - jnp.max(probs, axis=-1, keepdims=True))
    probs = probs / jnp.sum(probs, axis=-1, keepdims=True)
    prob_first = jnp.sum(probs * first_hot, axis=-1, keepdims=True)
    prob_second = jnp.sum(probs * second_hot, axis=-1, keepdims=True)
    gate = (prob_first * first_hot + prob_second * second_hot) / (prob_first + prob_second)
    combine = jnp.zeros((tok, lanes), F32)
    for k in range(experts):
        combine = combine + jnp.where(expert_of == k, gate[:, k : k + 1], 0.0)
    combine = (combine * placing)[:, 0:n_slots]
    high = combine.astype(BF)
    low = (combine - high.astype(F32)).astype(BF)

    early[4].wait()
    learner_in = student[0]
    shifted = learner_in - jnp.max(learner_in, axis=-1, keepdims=True)
    learner = shifted - jnp.log(jnp.sum(jnp.exp(shifted), axis=-1, keepdims=True))
    target_col = column(targets[0:1, :])
    vocab = student.shape[2]
    picked = lax.broadcasted_iota(jnp.int32, (tok, vocab), 1).astype(F32) == target_col
    hit = jnp.sum(jnp.where(picked, learner, 0.0), axis=-1, keepdims=True)
    loads[2].wait()

    for h in range(2):
        part = halves[h]
        for k in hop_order:
            count(cap * half_width, rz_r.at[2 * k + h])
            z_all[k * main : (k + 1) * main, part] = z_a[k, :, part]
            z_stage[k * rest : (k + 1) * rest, part] = z_b[k, :, part].astype(F32)
        z_all[n_main:, part] = z_stage[:, part].astype(BF)
        back = z_all[:, part]
        moe = jnp.dot(high, back, preferred_element_type=F32) + jnp.dot(
            low, back, preferred_element_type=F32
        )
        out_stage[:, part] = (mid[:, part] + moe).astype(BF)
    out = out_stage[...]
    out_copy = pltpu.make_async_copy(out_stage, layer_out.at[0], wsem.at[8])
    out_copy.start()

    final = layer_norm(out.astype(F32), gains[2]).astype(BF)
    logits = jnp.dot(final, short[...], preferred_element_type=F32)
    logits = logits - jnp.max(logits, axis=-1, keepdims=True)
    teacher = logits - jnp.log(jnp.sum(jnp.exp(logits), axis=-1, keepdims=True))
    token_loss = jnp.sum(jnp.exp(teacher) * (teacher - learner), axis=-1, keepdims=True) - hit
    counted = jnp.where(is_decoder, valid, 0.0)
    loss_sum = jnp.sum(token_loss * counted, axis=0, keepdims=True)
    loss_count = jnp.sum(counted, axis=0, keepdims=True)
    spot = lax.broadcasted_iota(jnp.int32, lsend.shape, 1)
    pair = jnp.where(spot == 0, loss_sum, jnp.where(spot == 1, loss_count, 0.0))
    lsend[...] = pair

    mine = (seg - half_seg) * n_exp + me
    n_loss = (n_seg - half_seg) * n_exp

    @pl.when(is_decoder)
    def _():
        lrecv[mine] = pair
        for ds in range(n_seg):
            for d in range(n_exp):
                if ds or d:
                    pltpu.make_async_remote_copy(
                        lsend, lrecv.at[mine], l_s, l_r,
                        device_id=peer(ds, d), device_id_type=MESH,
                    ).start()
        landed(lrecv.at[0 : n_loss - 1], l_r)

    @pl.when(seg < half_seg)
    def _():
        landed(lrecv, l_r)

    total = lrecv[0]
    for i in range(1, (n_seg - half_seg) * n_exp):
        total = total + lrecv[i]
    loss_out[...] = total[0:1, 0:1] / total[0:1, 1:2]

    @pl.when(is_decoder)
    def _():
        landed(lwide.at[0 : n_seg * n_exp - 1], l_s)

    out_copy.wait()
    moved = 2 * cap * (experts - 1 + (2 * gx - 1) * experts)
    left = moved * width // units
    while left:
        step = min(left, win.shape[0])
        landed(win.at[0:step], sent)
        left -= step

    @pl.when(seg < half_seg)
    def _():
        landed(kmem, msem.at[2])
        len_copy.wait_send()


def local(
    hidden, memory, lengths, memory_lengths, routes, norm_gain, router,
    w_in, w_out, shortlist, student, targets,
):
    n_seg = lax.axis_size("segment")
    n_exp = lax.axis_size("expert")
    experts = router.shape[2]
    group = n_exp // experts
    gc = 2
    gx = group // gc
    tok, width = hidden.shape[1], hidden.shape[2]
    units = w_in.shape[2]
    vocab = shortlist.shape[2]
    cap = 5 * tok // 8
    main = cap // 16 * 16
    rest = cap - main
    blocks = gx * experts
    vm = pl.BlockSpec(memory_space=pltpu.VMEM)
    hbm = pl.BlockSpec(memory_space=pl.ANY)
    v = pltpu.VMEM
    dma = pltpu.SemaphoreType.DMA
    nx = max(gx - 1, 1) * experts
    scratch = [
        v((1, tok, width), BF), v((1, 2, tok), jnp.int32), v((3, 1, width), F32),
        v((1, experts, width), BF), v((1, tok, vocab), F32), v((tok, width), BF),
        v((width, units), BF), v((units, width), BF), v((width, vocab), BF),
        v((tok, width), BF), v((8, 128), jnp.int32), v((8, 128), jnp.int32), v((tok, width), F32),
        v((experts, main, width), BF), v((experts, rest, width), BF),
        v((experts * gc * gx * cap, width), BF), v((gc * blocks, rest, width), BF),
        v((gx * rest, width), F32), v((experts, gc * gx * cap, units), BF),
        v((experts, gx * cap, width), F32),
        v((experts, gx * cap, width), BF), v((experts, gx * cap, width), BF),
        v((nx, main, width), BF), v((nx, rest, width), BF),
        v((nx, main, width), BF), v((nx, rest, width), BF),
        v((experts, main, width), BF), v((experts, rest, width), BF),
        v((experts, main, width), BF), v((experts, rest, width), BF),
        v((experts * cap, width), BF), v((experts * rest, width), F32),
        v((1, 128), F32), v(((n_seg - n_seg // 2) * n_exp, 1, 128), F32),
        v((n_seg * n_exp, 1, 128), F32), v((cap * width // 1024, 8, 128), BF),
        dma((9,)), dma((7,)), dma((2 * blocks,)), dma((blocks,)),
        dma((2 * experts,)), dma((2 * nx,)), dma((2 * experts,)),
        dma(()), dma(()), dma(()), pltpu.SemaphoreType.REGULAR((max(experts - 2, 1),)),
    ]
    layer_out, loss = pl.pallas_call(
        functools.partial(kernel, n_seg, n_exp, experts, gx, gc),
        out_shape=(
            jax.ShapeDtypeStruct((1, tok, width), BF),
            jax.ShapeDtypeStruct((1, 1), F32),
        ),
        in_specs=[hbm, hbm, vm, vm, hbm, hbm, hbm, hbm, hbm, hbm, hbm, vm],
        out_specs=(hbm, vm),
        scratch_shapes=scratch,
        compiler_params=pltpu.CompilerParams(
            collective_id=0, has_side_effects=True, vmem_limit_bytes=60 * 1024 * 1024
        ),
    )(
        hidden, memory, lengths, memory_lengths, jnp.swapaxes(routes, 1, 2),
        jnp.swapaxes(norm_gain, 0, 1), jnp.swapaxes(router, 1, 2),
        w_in, w_out, shortlist, student, targets,
    )
    return layer_out, loss[0, 0]


def solution(mesh):
    placed = (
        P("segment", "expert", None),
        P("segment", "expert", None),
        P("segment", "expert"),
        P("segment", "expert"),
        P("segment", "expert", None),
        P("segment", None, None),
        P("segment", None, None),
        P("segment", None, "expert"),
        P("segment", "expert", None),
        P("segment", None, None),
        P("segment", "expert", None),
        P("segment", "expert"),
    )
    return jax.shard_map(
        local,
        mesh=mesh,
        in_specs=placed,
        out_specs=(P("segment", "expert", None), P()),
        check_vma=False,
    )
```

```python
import functools
import math

import jax
import jax.numpy as jnp
from jax import lax
from jax.experimental import pallas as pl
from jax.experimental.pallas import tpu as pltpu
from jax.sharding import PartitionSpec as P

HEAD_DIM = 128
LEN = 32
EPS = 1e-05
MESH = pl.DeviceIdType.MESH
BF = jnp.bfloat16
F32 = jnp.float32


def layer_norm(values, gain_row):
    centred = values - jnp.mean(values, axis=-1, keepdims=True)
    spread = jnp.mean(centred * centred, axis=-1, keepdims=True)
    return centred * lax.rsqrt(spread + EPS) * gain_row


def xor(a, k, count):
    out = 0
    bit = 1
    while bit < count:
        out = out + lax.rem(a // bit + (k // bit) % 2, 2) * bit
        bit *= 2
    return out


def kernel(
    n_seg, n_exp, experts, gx, gc,
    hidden_any, memory, lengths, memory_lengths, routes_any, gain_any, router_any,
    w_in, w_out, shortlist, student_any, targets,
    layer_out, loss_out,
    hidden, routes, norm_gain, router, student, out_stage,
    win, wout, short, kmem, klen_src, klen, mid,
    out_a, out_b, x, x_b, stage, act, y0,
    core, rc, xs_a, xs_b, rx_a, rx_b, zs_a, zs_b, z_a, z_b, z_all, z_stage,
    lsend, lrecv, lwide, tally,
    wsem, msem, ra, rb, rc_r, rx_r, rz_r, sent, l_s, l_r, met,
):
    seg = lax.axis_index("segment")
    me = lax.axis_index("expert")
    half_seg = n_seg // 2
    group = gx * gc
    e = me // group
    j = lax.rem(me, group)
    xi = j // gc
    ci = lax.rem(j, gc)
    tok = hidden.shape[1]
    width = hidden.shape[2]
    heads = width // HEAD_DIM
    cap = 5 * tok // 8
    main = cap // 16 * 16
    rest = cap - main
    hop_order = list(range(1, experts))

    def peer(ds, d):
        return (lax.rem(seg + ds, n_seg), lax.rem(me + d, n_exp))

    def dev(e2, x2, c2):
        return (seg, (e2 * gx + x2) * gc + c2)

    barrier = pltpu.get_barrier_semaphore()
    to_seg = lax.rem(seg + half_seg, n_seg)
    sides = [((e > 0), (lax.rem(e + experts - 1, experts))), ((e < experts - 1), lax.rem(e + 1, experts))]
    beside = (e > 0).astype(jnp.int32) + (e < experts - 1).astype(jnp.int32)

    def greet(sem):
        for there, e2 in sides:
            @pl.when(there)
            def _():
                pl.semaphore_signal(sem, inc=1, device_id=dev(e2, xi, ci), device_id_type=MESH)

    near = [(to_seg, me)]
    near += [dev(e, lax.rem(xi + d, gx), ci) for d in range(1, gx)]
    near += [dev(e, xi, lax.rem(ci + d, gc)) for d in range(1, gc)]
    for device in near:
        pl.semaphore_signal(barrier, inc=1, device_id=device, device_id_type=MESH)
    greet(barrier)

    early = [
        pltpu.make_async_copy(hidden_any, hidden, wsem.at[3]),
        pltpu.make_async_copy(gain_any, norm_gain, wsem.at[4]),
        pltpu.make_async_copy(routes_any, routes, wsem.at[5]),
        pltpu.make_async_copy(router_any, router, wsem.at[6]),
        pltpu.make_async_copy(student_any, student, wsem.at[7]),
    ]
    for load in early:
        load.start()
    loads = [
        pltpu.make_async_copy(w_in.at[0], win, wsem.at[0]),
        pltpu.make_async_copy(w_out.at[0], wout, wsem.at[1]),
        pltpu.make_async_copy(shortlist.at[0], short, wsem.at[2]),
    ]
    klen_src[...] = jnp.broadcast_to(memory_lengths[0:1, 0:1], klen_src.shape)
    for q in range(1, tok // LEN):
        klen_src[q : q + 1, :] = jnp.broadcast_to(memory_lengths[0:1, q : q + 1], (1, 128))
    pl.semaphore_wait(barrier, len(near) + beside)

    is_decoder = seg >= half_seg
    groups = 4
    band = width // groups
    mem_copies = [
        pltpu.make_async_remote_copy(
            memory.at[0, :, g * band : (g + 1) * band], kmem.at[:, g * band : (g + 1) * band],
            msem.at[2], msem.at[3 + g], device_id=(to_seg, me), device_id_type=MESH,
        )
        for g in range(groups)
    ]
    len_copy = pltpu.make_async_remote_copy(
        klen_src, klen, msem.at[0], msem.at[1], device_id=(to_seg, me), device_id_type=MESH
    )

    @pl.when(seg < half_seg)
    def _():
        len_copy.start()
        for copy in mem_copies:
            copy.start()

    for load in loads:
        load.start()

    rounds = max(experts - 2, 0)
    if rounds:
        greet(met.at[0])
    early[0].wait()
    early[1].wait()
    gains = [norm_gain[i] for i in range(3)]
    states = hidden[0].astype(F32)

    queries = layer_norm(states, gains[0]).astype(BF)
    for i in range(rounds - 1):
        pl.semaphore_wait(met.at[i], beside)
        greet(met.at[i + 1])

    early[2].wait()
    expert_lane = lax.broadcasted_iota(jnp.int32, (tok, experts), 1)
    pos = lax.broadcasted_iota(jnp.int32, (tok, 1), 0)
    valid = jnp.zeros((tok, 1), F32)
    for q in range(tok // LEN):
        ok = (pos >= q * LEN) & (pos < (q + 1) * LEN) & (pos - q * LEN < lengths[0:1, q : q + 1])
        valid = valid + ok.astype(F32)
    square = lax.broadcasted_iota(jnp.int32, (tok, tok), 0) == lax.broadcasted_iota(
        jnp.int32, (tok, tok), 1
    )

    def column(row):
        spread = jnp.where(square, jnp.broadcast_to(row, (tok, tok)), 0)
        return jnp.sum(spread.astype(F32), axis=-1, keepdims=True)

    expert_lane = expert_lane.astype(F32)
    first_hot = (column(routes[0, 0:1, :]) == expert_lane).astype(F32)
    second_hot = (column(routes[0, 1:2, :]) == expert_lane).astype(F32)
    chosen = (first_hot + second_hot) * valid
    before = (
        lax.broadcasted_iota(jnp.int32, (tok, tok), 1)
        < lax.broadcasted_iota(jnp.int32, (tok, tok), 0)
    ).astype(BF)
    rank = jnp.dot(before, chosen.astype(BF), preferred_element_type=F32)
    n_main = experts * main
    n_slots = experts * cap
    lanes = -(-n_slots // 128) * 128
    lane = lax.broadcasted_iota(jnp.int32, (1, lanes), 1)
    slot_of = jnp.full((1, lanes), -1, jnp.int32)
    expert_of = jnp.full((1, lanes), -1, jnp.int32)
    for k in range(experts):
        ek = xor(e, k, experts)
        in_main = (lane >= k * main) & (lane < (k + 1) * main)
        low = n_main + k * rest
        in_rest = (lane >= low) & (lane < low + rest)
        slot_of = jnp.where(in_main, lane - k * main, slot_of)
        slot_of = jnp.where(in_rest, lane - low + main, slot_of)
        expert_of = jnp.where(in_main | in_rest, ek, expert_of)
    placing = jnp.zeros((tok, lanes), F32)
    for k in range(experts):
        here = (expert_of == k) & (rank[:, k : k + 1] == slot_of.astype(F32))
        placing = placing + jnp.where(here, chosen[:, k : k + 1], 0.0)
    place_rows = jnp.transpose(placing)[0:n_slots].astype(BF)
    @pl.when(seg < half_seg)
    def _():
        mid[...] = states

    @pl.when(seg >= half_seg)
    def _():
        len_copy.wait_recv()
        col = lax.broadcasted_iota(jnp.int32, (tok, tok), 1)
        row = lax.broadcasted_iota(jnp.int32, (tok, tok), 0)
        klen_v = klen[...]
        allowed = jnp.zeros((tok, tok), jnp.bool_)
        for q in range(tok // LEN):
            inside = (col >= q * LEN) & (col - q * LEN < klen_v[q : q + 1, 0:1])
            inside = inside & (col < (q + 1) * LEN) & (row >= q * LEN) & (row < (q + 1) * LEN)
            allowed = allowed | inside
        for g in range(groups):
            mem_copies[g].wait_recv()
            keys = kmem[:, g * band : (g + 1) * band]
            parts = [slice(h * HEAD_DIM, (h + 1) * HEAD_DIM) for h in range(band // HEAD_DIM)]
            scores = jnp.concatenate(
                [
                    jnp.where(
                        allowed,
                        lax.dot_general(
                            queries[:, g * band + part.start : g * band + part.stop], keys[:, part],
                            (((1,), (1,)), ((), ())), preferred_element_type=F32,
                        )
                        * (1.0 / math.sqrt(HEAD_DIM)),
                        -1e30,
                    )
                    for part in parts
                ],
                axis=0,
            )
            top = jnp.max(scores, axis=-1, keepdims=True)
            raised = jnp.exp(scores - top)
            weights = (raised / jnp.sum(raised, axis=-1, keepdims=True)).astype(BF)
            for h, part in enumerate(parts):
                here = slice(g * band + part.start, g * band + part.stop)
                mid[:, here] = states[:, here] + jnp.dot(
                    weights[h * tok : (h + 1) * tok], keys[:, part], preferred_element_type=F32
                )

    if rounds:
        pl.semaphore_wait(met.at[rounds - 1], beside)

    normed = layer_norm(mid[...], gains[1]).astype(BF)

    slots = jnp.dot(place_rows, normed, preferred_element_type=F32)

    chunk = gc * gx * cap
    side = gx * cap
    side_main = gx * main
    half_width = width // 2
    halves = [slice(h * half_width, (h + 1) * half_width) for h in range(2)]

    def rows_a(dc, dx, k):
        return pl.ds(k * chunk + dc * side + dx * main, main)

    def index_b(dc, dx, k):
        return (dc * gx + dx) * experts + k

    for k in hop_order:
        out_a[k] = slots[k * main : (k + 1) * main].astype(BF)
        out_b[k] = slots[n_main + k * rest : n_main + (k + 1) * rest].astype(BF)
    x[rows_a(0, 0, 0), :] = slots[0:main].astype(BF)
    x_b[0] = slots[n_main : n_main + rest].astype(BF)

    def send(src, dst, r_sem, target):
        pltpu.make_async_remote_copy(
            src, dst, sent, r_sem, device_id=target, device_id_type=MESH
        ).start()

    def landed(ref, sem):
        pltpu.make_async_copy(ref, ref, sem).wait()

    def count(size, sem):
        landed(tally.at[0 : size // 1024], sem)

    def piece(slot, p):
        if p == 0:
            return x.at[rows_a(*slot), :]
        return x_b.at[index_b(*slot)]

    def mark(slot, p):
        if slot[0]:
            return rb.at[slot[1] * experts + slot[2]]
        return ra.at[slot[1] * experts + slot[2]]

    def arrived(slot, p):
        if p == 0:
            count(cap * width, mark(slot, 0))

    def forward(slot_from, slot_to, p, target):
        send(piece(slot_from, p), piece(slot_to, p), mark(slot_to, p), target)

    def to_plane(k):
        target = dev(xor(e, k, experts), xi, ci)
        for p in range(2):
            src = out_b.at[k] if p else out_a.at[k]
            send(src, piece((0, 0, k), p), mark((0, 0, k), p), target)

    core_dev = dev(e, xi, lax.rem(ci + 1, gc))

    def from_column(k):
        for p in range(2):
            if k:
                arrived((0, 0, k), p)
            for d in range(1, gx):
                forward((0, 0, k), (0, d, k), p, dev(e, lax.rem(xi + d, gx), ci))
            forward((0, 0, k), (1, 0, k), p, core_dev)

    def from_chips(k):
        for p in range(2):
            for d in range(1, gx):
                arrived((0, d, k), p)
                forward((0, d, k), (1, d, k), p, core_dev)

    units = win.shape[1]
    tile = min(1024, units)
    tile2 = min(1024, half_width)

    def first(k):
        for d in range(0 if k else 1, gx):
            count(cap * width, mark((1, d, k), 0))
        for dc in range(gc):
            for d in range(gx):
                stage[d * rest : (d + 1) * rest, :] = x_b[index_b(dc, d, k)].astype(F32)
            low = k * chunk + dc * side + side_main
            x[low : low + gx * rest, :] = stage[...].astype(BF)
        if k == 0:
            loads[0].wait()
        rows = slice(k * chunk, (k + 1) * chunk)

        @pl.loop(0, units // tile)
        def _(i):
            cols = pl.ds(pl.multiple_of(i * tile, tile), tile)
            act[k, :, cols] = jnp.maximum(
                jnp.dot(x[rows, :], win[:, cols], preferred_element_type=F32), 0.0
            ).astype(BF)

    def second(k):
        if k == 0:
            loads[1].wait()
        for h in range(2):
            @pl.loop(0, half_width // tile2)
            def _(i):
                cols = pl.ds(pl.multiple_of(h * half_width + i * tile2, tile2), tile2)
                part = jnp.dot(act[k], wout[:, cols], preferred_element_type=F32)
                core[k, :, cols] = part[side:].astype(BF)
                y0[k, :, cols] = part[0:side]

            send(core.at[k, :, halves[h]], rc.at[k, :, halves[h]], rc_r.at[2 * k + h], core_dev)

    def to_chips(k):
        for h in range(2):
            part = halves[h]
            landed(rc.at[k, :, part], rc_r.at[2 * k + h])
            tail = y0[k, side_main:, part] + rc[k, side_main:, part].astype(F32)
            for d in range(1, gx):
                o = (d - 1) * experts + k
                rows = slice(d * main, (d + 1) * main)
                xs_a[o, :, part] = (y0[k, rows, part] + rc[k, rows, part].astype(F32)).astype(BF)
                xs_b[o, :, part] = tail[d * rest : (d + 1) * rest].astype(BF)
                target = dev(e, lax.rem(xi + gx - d, gx), ci)
                for src, dst in [(xs_a, rx_a), (xs_b, rx_b)]:
                    send(src.at[o, :, part], dst.at[o, :, part], rx_r.at[2 * o + h], target)

    def to_column(k):
        for h in range(2):
            part = halves[h]
            sum_a = y0[k, 0:main, part] + rc[k, 0:main, part].astype(F32)
            tail = y0[k, side_main:, part] + rc[k, side_main:, part].astype(F32)
            sum_b = tail[0:rest]
            for d in range(1, gx):
                o = (d - 1) * experts + k
                count(cap * half_width, rx_r.at[2 * o + h])
                sum_a = sum_a + rx_a[o, :, part].astype(F32)
                sum_b = sum_b + rx_b[o, :, part].astype(F32)
            if k:
                zs_a[k, :, part] = sum_a.astype(BF)
                zs_b[k, :, part] = sum_b.astype(BF)
                target = dev(xor(e, k, experts), xi, ci)
                for src, dst in [(zs_a, z_a), (zs_b, z_b)]:
                    send(src.at[k, :, part], dst.at[k, :, part], rz_r.at[2 * k + h], target)
            else:
                z_all[0:main, part] = sum_a.astype(BF)
                z_stage[0:rest, part] = sum_b

    last = experts - 1

    def relay(core_side, steps):
        steps = [(step, k) for step, k in steps if k <= last]
        if steps:
            @pl.when((ci > 0) if core_side else (ci == 0))
            def _():
                for step, k in steps:
                    step(k)

    def do(*steps):
        for step, k in steps:
            if k <= last:
                step(k)

    later = range(4, experts)
    do((to_plane, 2))
    from_column(0)

    def beside_core(k):
        count(cap * width, mark((1, 0, k), 0))

    relay(1, [(beside_core, 0), (to_plane, 3), (to_plane, 1)])
    from_chips(0)
    relay(0, [(to_plane, 3), (to_plane, 1), (beside_core, 0)])
    do(*[(to_plane, k) for k in later], (from_column, 2))
    first(0)
    relay(1, [(from_column, 3)])
    second(0)
    relay(0, [(from_column, 3), (from_chips, 2), (from_column, 1)])
    relay(1, [(from_column, 1), (from_chips, 2)])
    do((first, 2))
    relay(1, [(from_chips, 3)])
    do((second, 2))
    relay(0, [(from_chips, 3)])
    relay(1, [(from_chips, 1)])
    do((to_chips, 2), (to_chips, 0), (first, 3))
    relay(0, [(from_chips, 1)])
    do((second, 3), (first, 1), (to_chips, 3), (to_column, 2), (second, 1), (to_chips, 1))
    for k in later:
        do((from_column, k), (from_chips, k), (first, k), (second, k), (to_chips, k))
    do((to_column, 3))
    early[3].wait()
    probs = lax.dot_general(
        normed, router[0], (((1,), (1,)), ((), ())), preferred_element_type=F32
    )
    probs = jnp.exp(probs - jnp.max(probs, axis=-1, keepdims=True))
    probs = probs / jnp.sum(probs, axis=-1, keepdims=True)
    prob_first = jnp.sum(probs * first_hot, axis=-1, keepdims=True)
    prob_second = jnp.sum(probs * second_hot, axis=-1, keepdims=True)
    gate = (prob_first * first_hot + prob_second * second_hot) / (prob_first + prob_second)
    combine = jnp.zeros((tok, lanes), F32)
    for k in range(experts):
        combine = combine + jnp.where(expert_of == k, gate[:, k : k + 1], 0.0)
    combine = (combine * placing)[:, 0:n_slots]
    high = combine.astype(BF)
    low = (combine - high.astype(F32)).astype(BF)

    do((to_column, 1))
    early[4].wait()
    learner_in = student[0]
    shifted = learner_in - jnp.max(learner_in, axis=-1, keepdims=True)
    learner = shifted - jnp.log(jnp.sum(jnp.exp(shifted), axis=-1, keepdims=True))
    target_col = column(targets[0:1, :])
    vocab = student.shape[2]
    picked = lax.broadcasted_iota(jnp.int32, (tok, vocab), 1).astype(F32) == target_col
    hit = jnp.sum(jnp.where(picked, learner, 0.0), axis=-1, keepdims=True)
    loads[2].wait()

    to_column(0)
    for k in later:
        to_column(k)

    for h in range(2):
        part = halves[h]
        for k in hop_order:
            count(cap * half_width, rz_r.at[2 * k + h])
            z_all[k * main : (k + 1) * main, part] = z_a[k, :, part]
            z_stage[k * rest : (k + 1) * rest, part] = z_b[k, :, part].astype(F32)
        z_all[n_main:, part] = z_stage[:, part].astype(BF)
        back = z_all[:, part]
        moe = jnp.dot(high, back, preferred_element_type=F32) + jnp.dot(
            low, back, preferred_element_type=F32
        )
        out_stage[:, part] = (mid[:, part] + moe).astype(BF)
    out = out_stage[...]
    out_copy = pltpu.make_async_copy(out_stage, layer_out.at[0], wsem.at[8])
    out_copy.start()

    final = layer_norm(out.astype(F32), gains[2]).astype(BF)
    logits = jnp.dot(final, short[...], preferred_element_type=F32)
    logits = logits - jnp.max(logits, axis=-1, keepdims=True)
    teacher = logits - jnp.log(jnp.sum(jnp.exp(logits), axis=-1, keepdims=True))
    token_loss = jnp.sum(jnp.exp(teacher) * (teacher - learner), axis=-1, keepdims=True) - hit
    counted = jnp.where(is_decoder, valid, 0.0)
    loss_sum = jnp.sum(token_loss * counted, axis=0, keepdims=True)
    loss_count = jnp.sum(counted, axis=0, keepdims=True)
    spot = lax.broadcasted_iota(jnp.int32, lsend.shape, 1)
    pair = jnp.where(spot == 0, loss_sum, jnp.where(spot == 1, loss_count, 0.0))
    lsend[...] = pair

    mine = (seg - half_seg) * n_exp + me
    n_loss = (n_seg - half_seg) * n_exp

    @pl.when(is_decoder)
    def _():
        lrecv[mine] = pair
        for ds in reversed(range(n_seg)):
            for d in range(n_exp):
                if ds or d:
                    pltpu.make_async_remote_copy(
                        lsend, lrecv.at[mine], l_s, l_r,
                        device_id=peer(ds, d), device_id_type=MESH,
                    ).start()
        landed(lrecv.at[0 : n_loss - 1], l_r)

    @pl.when(seg < half_seg)
    def _():
        landed(lrecv, l_r)

    total = lrecv[0]
    for i in range(1, (n_seg - half_seg) * n_exp):
        total = total + lrecv[i]
    loss_out[...] = total[0:1, 0:1] / total[0:1, 1:2]

    @pl.when(is_decoder)
    def _():
        landed(lwide.at[0 : n_seg * n_exp - 1], l_s)

    out_copy.wait()
    moved = 2 * cap * (experts - 1 + (2 * gx - 1) * experts)
    left = moved * width // units
    while left:
        step = min(left, win.shape[0])
        landed(win.at[0:step], sent)
        left -= step

    @pl.when(seg < half_seg)
    def _():
        landed(kmem, msem.at[2])
        len_copy.wait_send()


def local(
    hidden, memory, lengths, memory_lengths, routes, norm_gain, router,
    w_in, w_out, shortlist, student, targets,
):
    n_seg = lax.axis_size("segment")
    n_exp = lax.axis_size("expert")
    experts = router.shape[2]
    group = n_exp // experts
    gc = 2
    gx = group // gc
    tok, width = hidden.shape[1], hidden.shape[2]
    units = w_in.shape[2]
    vocab = shortlist.shape[2]
    cap = 5 * tok // 8
    main = cap // 16 * 16
    rest = cap - main
    blocks = gx * experts
    vm = pl.BlockSpec(memory_space=pltpu.VMEM)
    hbm = pl.BlockSpec(memory_space=pl.ANY)
    v = pltpu.VMEM
    dma = pltpu.SemaphoreType.DMA
    nx = max(gx - 1, 1) * experts
    scratch = [
        v((1, tok, width), BF), v((1, 2, tok), jnp.int32), v((3, 1, width), F32),
        v((1, experts, width), BF), v((1, tok, vocab), F32), v((tok, width), BF),
        v((width, units), BF), v((units, width), BF), v((width, vocab), BF),
        v((tok, width), BF), v((8, 128), jnp.int32), v((8, 128), jnp.int32), v((tok, width), F32),
        v((experts, main, width), BF), v((experts, rest, width), BF),
        v((experts * gc * gx * cap, width), BF), v((gc * blocks, rest, width), BF),
        v((gx * rest, width), F32), v((experts, gc * gx * cap, units), BF),
        v((experts, gx * cap, width), F32),
        v((experts, gx * cap, width), BF), v((experts, gx * cap, width), BF),
        v((nx, main, width), BF), v((nx, rest, width), BF),
        v((nx, main, width), BF), v((nx, rest, width), BF),
        v((experts, main, width), BF), v((experts, rest, width), BF),
        v((experts, main, width), BF), v((experts, rest, width), BF),
        v((experts * cap, width), BF), v((experts * rest, width), F32),
        v((1, 128), F32), v(((n_seg - n_seg // 2) * n_exp, 1, 128), F32),
        v((n_seg * n_exp, 1, 128), F32), v((cap * width // 1024, 8, 128), BF),
        dma((9,)), dma((7,)), dma((blocks,)), dma((blocks,)),
        dma((2 * experts,)), dma((2 * nx,)), dma((2 * experts,)),
        dma(()), dma(()), dma(()), pltpu.SemaphoreType.REGULAR((max(experts - 2, 1),)),
    ]
    layer_out, loss = pl.pallas_call(
        functools.partial(kernel, n_seg, n_exp, experts, gx, gc),
        out_shape=(
            jax.ShapeDtypeStruct((1, tok, width), BF),
            jax.ShapeDtypeStruct((1, 1), F32),
        ),
        in_specs=[hbm, hbm, vm, vm, hbm, hbm, hbm, hbm, hbm, hbm, hbm, vm],
        out_specs=(hbm, vm),
        scratch_shapes=scratch,
        compiler_params=pltpu.CompilerParams(
            collective_id=0, has_side_effects=True, vmem_limit_bytes=60 * 1024 * 1024
        ),
    )(
        hidden, memory, lengths, memory_lengths, jnp.swapaxes(routes, 1, 2),
        jnp.swapaxes(norm_gain, 0, 1), jnp.swapaxes(router, 1, 2),
        w_in, w_out, shortlist, student, targets,
    )
    return layer_out, loss[0, 0]


def solution(mesh):
    placed = (
        P("segment", "expert", None),
        P("segment", "expert", None),
        P("segment", "expert"),
        P("segment", "expert"),
        P("segment", "expert", None),
        P("segment", None, None),
        P("segment", None, None),
        P("segment", None, "expert"),
        P("segment", "expert", None),
        P("segment", None, None),
        P("segment", "expert", None),
        P("segment", "expert"),
    )
    return jax.shard_map(
        local,
        mesh=mesh,
        in_specs=placed,
        out_specs=(P("segment", "expert", None), P()),
        check_vma=False,
    )
```

```python
import functools
import math

import jax
import jax.numpy as jnp
from jax import lax
from jax.experimental import pallas as pl
from jax.experimental.pallas import tpu as pltpu
from jax.sharding import PartitionSpec as P

HEAD_DIM = 128
LEN = 32
EPS = 1e-05
MESH = pl.DeviceIdType.MESH
BF = jnp.bfloat16
F32 = jnp.float32


def layer_norm(values, gain_row):
    centred = values - jnp.mean(values, axis=-1, keepdims=True)
    spread = jnp.mean(centred * centred, axis=-1, keepdims=True)
    return centred * lax.rsqrt(spread + EPS) * gain_row


def xor(a, k, count):
    out = 0
    bit = 1
    while bit < count:
        out = out + lax.rem(a // bit + (k // bit) % 2, 2) * bit
        bit *= 2
    return out


def kernel(
    n_seg, n_exp, experts, gx, gc,
    hidden_any, memory, lengths, memory_lengths, routes_any, gain_any, router_any,
    w_in, w_out, shortlist, student_any, targets,
    layer_out, loss_out,
    hidden, routes, norm_gain, router, student, out_stage,
    win, wout, short, kmem, klen_src, klen, mid,
    out_a, out_b, x, x_b, stage, act, y0,
    core, rc, xs_a, xs_b, rx_a, rx_b, zs_a, zs_b, z_a, z_b, z_all, z_stage,
    lsend, lrecv, lwide, tally,
    wsem, msem, ra, rb, rc_r, rx_r, rz_r, sent, l_s, l_r, met,
):
    seg = lax.axis_index("segment")
    me = lax.axis_index("expert")
    half_seg = n_seg // 2
    group = gx * gc
    e = me // group
    j = lax.rem(me, group)
    xi = j // gc
    ci = lax.rem(j, gc)
    tok = hidden.shape[1]
    width = hidden.shape[2]
    heads = width // HEAD_DIM
    cap = 5 * tok // 8
    main = cap // 16 * 16
    rest = cap - main
    hop_order = list(range(1, experts))

    def peer(ds, d):
        return (lax.rem(seg + ds, n_seg), lax.rem(me + d, n_exp))

    def dev(e2, x2, c2):
        return (seg, (e2 * gx + x2) * gc + c2)

    barrier = pltpu.get_barrier_semaphore()
    to_seg = lax.rem(seg + half_seg, n_seg)
    sides = [((e > 0), (lax.rem(e + experts - 1, experts))), ((e < experts - 1), lax.rem(e + 1, experts))]
    beside = (e > 0).astype(jnp.int32) + (e < experts - 1).astype(jnp.int32)

    def greet(sem):
        for there, e2 in sides:
            @pl.when(there)
            def _():
                pl.semaphore_signal(sem, inc=1, device_id=dev(e2, xi, ci), device_id_type=MESH)

    near = [(to_seg, me)]
    near += [dev(e, lax.rem(xi + d, gx), ci) for d in range(1, gx)]
    near += [dev(e, xi, lax.rem(ci + d, gc)) for d in range(1, gc)]
    for device in near:
        pl.semaphore_signal(barrier, inc=1, device_id=device, device_id_type=MESH)
    greet(barrier)

    early = [
        pltpu.make_async_copy(hidden_any, hidden, wsem.at[3]),
        pltpu.make_async_copy(gain_any, norm_gain, wsem.at[4]),
        pltpu.make_async_copy(routes_any, routes, wsem.at[5]),
        pltpu.make_async_copy(router_any, router, wsem.at[6]),
        pltpu.make_async_copy(student_any, student, wsem.at[7]),
    ]
    for load in early:
        load.start()
    loads = [
        pltpu.make_async_copy(w_in.at[0], win, wsem.at[0]),
        pltpu.make_async_copy(w_out.at[0], wout, wsem.at[1]),
        pltpu.make_async_copy(shortlist.at[0], short, wsem.at[2]),
    ]
    klen_src[...] = jnp.broadcast_to(memory_lengths[0:1, 0:1], klen_src.shape)
    for q in range(1, tok // LEN):
        klen_src[q : q + 1, :] = jnp.broadcast_to(memory_lengths[0:1, q : q + 1], (1, 128))
    pl.semaphore_wait(barrier, len(near) + beside)

    is_decoder = seg >= half_seg
    groups = 2
    band = width // groups
    mem_copies = [
        pltpu.make_async_remote_copy(
            memory.at[0, :, g * band : (g + 1) * band], kmem.at[:, g * band : (g + 1) * band],
            msem.at[2], msem.at[3 + g], device_id=(to_seg, me), device_id_type=MESH,
        )
        for g in range(groups)
    ]
    len_copy = pltpu.make_async_remote_copy(
        klen_src, klen, msem.at[0], msem.at[1], device_id=(to_seg, me), device_id_type=MESH
    )

    @pl.when(seg < half_seg)
    def _():
        len_copy.start()
        for copy in mem_copies:
            copy.start()

    for load in loads:
        load.start()

    rounds = max(experts - 2, 0)
    if rounds:
        greet(met.at[0])
    early[0].wait()
    early[1].wait()
    gains = [norm_gain[i] for i in range(3)]
    states = hidden[0].astype(F32)

    queries = layer_norm(states, gains[0]).astype(BF)
    for i in range(rounds - 1):
        pl.semaphore_wait(met.at[i], beside)
        greet(met.at[i + 1])

    early[2].wait()
    expert_lane = lax.broadcasted_iota(jnp.int32, (tok, experts), 1)
    pos = lax.broadcasted_iota(jnp.int32, (tok, 1), 0)
    valid = jnp.zeros((tok, 1), F32)
    for q in range(tok // LEN):
        ok = (pos >= q * LEN) & (pos < (q + 1) * LEN) & (pos - q * LEN < lengths[0:1, q : q + 1])
        valid = valid + ok.astype(F32)
    square = lax.broadcasted_iota(jnp.int32, (tok, tok), 0) == lax.broadcasted_iota(
        jnp.int32, (tok, tok), 1
    )

    def column(row):
        spread = jnp.where(square, jnp.broadcast_to(row, (tok, tok)), 0)
        return jnp.sum(spread.astype(F32), axis=-1, keepdims=True)

    expert_lane = expert_lane.astype(F32)
    first_hot = (column(routes[0, 0:1, :]) == expert_lane).astype(F32)
    second_hot = (column(routes[0, 1:2, :]) == expert_lane).astype(F32)
    chosen = (first_hot + second_hot) * valid
    before = (
        lax.broadcasted_iota(jnp.int32, (tok, tok), 1)
        < lax.broadcasted_iota(jnp.int32, (tok, tok), 0)
    ).astype(BF)
    rank = jnp.dot(before, chosen.astype(BF), preferred_element_type=F32)
    n_main = experts * main
    n_slots = experts * cap
    lanes = -(-n_slots // 128) * 128
    lane = lax.broadcasted_iota(jnp.int32, (1, lanes), 1)
    slot_of = jnp.full((1, lanes), -1, jnp.int32)
    expert_of = jnp.full((1, lanes), -1, jnp.int32)
    for k in range(experts):
        ek = xor(e, k, experts)
        in_main = (lane >= k * main) & (lane < (k + 1) * main)
        low = n_main + k * rest
        in_rest = (lane >= low) & (lane < low + rest)
        slot_of = jnp.where(in_main, lane - k * main, slot_of)
        slot_of = jnp.where(in_rest, lane - low + main, slot_of)
        expert_of = jnp.where(in_main | in_rest, ek, expert_of)
    placing = jnp.zeros((tok, lanes), F32)
    for k in range(experts):
        here = (expert_of == k) & (rank[:, k : k + 1] == slot_of.astype(F32))
        placing = placing + jnp.where(here, chosen[:, k : k + 1], 0.0)
    place_rows = jnp.transpose(placing)[0:n_slots].astype(BF)
    @pl.when(seg < half_seg)
    def _():
        mid[...] = states

    @pl.when(seg >= half_seg)
    def _():
        len_copy.wait_recv()
        col = lax.broadcasted_iota(jnp.int32, (tok, tok), 1)
        row = lax.broadcasted_iota(jnp.int32, (tok, tok), 0)
        klen_v = klen[...]
        allowed = jnp.zeros((tok, tok), jnp.bool_)
        for q in range(tok // LEN):
            inside = (col >= q * LEN) & (col - q * LEN < klen_v[q : q + 1, 0:1])
            inside = inside & (col < (q + 1) * LEN) & (row >= q * LEN) & (row < (q + 1) * LEN)
            allowed = allowed | inside
        for g in range(groups):
            mem_copies[g].wait_recv()
            keys = kmem[:, g * band : (g + 1) * band]
            parts = [slice(h * HEAD_DIM, (h + 1) * HEAD_DIM) for h in range(band // HEAD_DIM)]
            scores = jnp.concatenate(
                [
                    jnp.where(
                        allowed,
                        lax.dot_general(
                            queries[:, g * band + part.start : g * band + part.stop], keys[:, part],
                            (((1,), (1,)), ((), ())), preferred_element_type=F32,
                        )
                        * (1.0 / math.sqrt(HEAD_DIM)),
                        -1e30,
                    )
                    for part in parts
                ],
                axis=0,
            )
            top = jnp.max(scores, axis=-1, keepdims=True)
            raised = jnp.exp(scores - top)
            weights = (raised / jnp.sum(raised, axis=-1, keepdims=True)).astype(BF)
            for h, part in enumerate(parts):
                here = slice(g * band + part.start, g * band + part.stop)
                mid[:, here] = states[:, here] + jnp.dot(
                    weights[h * tok : (h + 1) * tok], keys[:, part], preferred_element_type=F32
                )

    if rounds:
        pl.semaphore_wait(met.at[rounds - 1], beside)

    normed = layer_norm(mid[...], gains[1]).astype(BF)

    slots = jnp.dot(place_rows, normed, preferred_element_type=F32)

    chunk = gc * gx * cap
    side = gx * cap
    side_main = gx * main
    half_width = width // 2
    halves = [slice(h * half_width, (h + 1) * half_width) for h in range(2)]

    def rows_a(dc, dx, k):
        return pl.ds(k * chunk + dc * side + dx * main, main)

    def index_b(dc, dx, k):
        return (dc * gx + dx) * experts + k

    for k in hop_order:
        out_a[k] = slots[k * main : (k + 1) * main].astype(BF)
        out_b[k] = slots[n_main + k * rest : n_main + (k + 1) * rest].astype(BF)
    x[rows_a(0, 0, 0), :] = slots[0:main].astype(BF)
    x_b[0] = slots[n_main : n_main + rest].astype(BF)

    def send(src, dst, r_sem, target):
        pltpu.make_async_remote_copy(
            src, dst, sent, r_sem, device_id=target, device_id_type=MESH
        ).start()

    def landed(ref, sem):
        pltpu.make_async_copy(ref, ref, sem).wait()

    def count(size, sem):
        landed(tally.at[0 : size // 1024], sem)

    def piece(slot, p):
        if p == 0:
            return x.at[rows_a(*slot), :]
        return x_b.at[index_b(*slot)]

    def mark(slot, p):
        if slot[0]:
            return rb.at[slot[2] + 1 if slot[1] or slot[2] else 0]
        return ra.at[slot[1] * experts + slot[2]]

    def arrived(slot, p):
        if p == 0:
            count(cap * width, mark(slot, 0))

    def forward(slot_from, slot_to, p, target):
        send(piece(slot_from, p), piece(slot_to, p), mark(slot_to, p), target)

    def to_plane(k):
        target = dev(xor(e, k, experts), xi, ci)
        for p in range(2):
            src = out_b.at[k] if p else out_a.at[k]
            send(src, piece((0, 0, k), p), mark((0, 0, k), p), target)

    core_dev = dev(e, xi, lax.rem(ci + 1, gc))

    def from_column(k):
        for p in range(2):
            if k:
                arrived((0, 0, k), p)
            for d in range(1, gx):
                forward((0, 0, k), (0, d, k), p, dev(e, lax.rem(xi + d, gx), ci))
            forward((0, 0, k), (1, 0, k), p, core_dev)

    def from_chips(k):
        for p in range(2):
            for d in range(1, gx):
                arrived((0, d, k), p)
                forward((0, d, k), (1, d, k), p, core_dev)

    units = win.shape[1]
    tile = min(1024, units)
    tile2 = min(1024, half_width)

    def first(k):
        count((gx if k else gx - 1) * cap * width, rb.at[k + 1])
        for dc in range(gc):
            for d in range(gx):
                stage[d * rest : (d + 1) * rest, :] = x_b[index_b(dc, d, k)].astype(F32)
            low = k * chunk + dc * side + side_main
            x[low : low + gx * rest, :] = stage[...].astype(BF)
        if k == 0:
            loads[0].wait()
        rows = slice(k * chunk, (k + 1) * chunk)

        @pl.loop(0, units // tile)
        def _(i):
            cols = pl.ds(pl.multiple_of(i * tile, tile), tile)
            act[k, :, cols] = jnp.maximum(
                jnp.dot(x[rows, :], win[:, cols], preferred_element_type=F32), 0.0
            ).astype(BF)

    def second(k):
        if k == 0:
            loads[1].wait()
        for h in range(2):
            @pl.loop(0, half_width // tile2)
            def _(i):
                cols = pl.ds(pl.multiple_of(h * half_width + i * tile2, tile2), tile2)
                part = jnp.dot(act[k], wout[:, cols], preferred_element_type=F32)
                core[k, :, cols] = part[side:].astype(BF)
                y0[k, :, cols] = part[0:side]

            send(core.at[k, :, halves[h]], rc.at[k, :, halves[h]], rc_r.at[2 * k + h], core_dev)

    def to_chips(k):
        for h in range(2):
            part = halves[h]
            landed(rc.at[k, :, part], rc_r.at[2 * k + h])
            tail = y0[k, side_main:, part] + rc[k, side_main:, part].astype(F32)
            for d in range(1, gx):
                o = (d - 1) * experts + k
                rows = slice(d * main, (d + 1) * main)
                xs_a[o, :, part] = (y0[k, rows, part] + rc[k, rows, part].astype(F32)).astype(BF)
                xs_b[o, :, part] = tail[d * rest : (d + 1) * rest].astype(BF)
                target = dev(e, lax.rem(xi + gx - d, gx), ci)
                for src, dst in [(xs_a, rx_a), (xs_b, rx_b)]:
                    send(src.at[o, :, part], dst.at[o, :, part], rx_r.at[2 * o + h], target)

    def to_column(k):
        for h in range(2):
            part = halves[h]
            sum_a = y0[k, 0:main, part] + rc[k, 0:main, part].astype(F32)
            tail = y0[k, side_main:, part] + rc[k, side_main:, part].astype(F32)
            sum_b = tail[0:rest]
            for d in range(1, gx):
                o = (d - 1) * experts + k
                count(cap * half_width, rx_r.at[2 * o + h])
                sum_a = sum_a + rx_a[o, :, part].astype(F32)
                sum_b = sum_b + rx_b[o, :, part].astype(F32)
            if k:
                zs_a[k, :, part] = sum_a.astype(BF)
                zs_b[k, :, part] = sum_b.astype(BF)
                target = dev(xor(e, k, experts), xi, ci)
                for src, dst in [(zs_a, z_a), (zs_b, z_b)]:
                    send(src.at[k, :, part], dst.at[k, :, part], rz_r.at[2 * k + h], target)
            else:
                z_all[0:main, part] = sum_a.astype(BF)
                z_stage[0:rest, part] = sum_b

    last = experts - 1

    def relay(core_side, steps):
        steps = [(step, k) for step, k in steps if k <= last]
        if steps:
            @pl.when((ci > 0) if core_side else (ci == 0))
            def _():
                for step, k in steps:
                    step(k)

    def do(*steps):
        for step, k in steps:
            if k <= last:
                step(k)

    later = range(4, experts)
    do((to_plane, 2))
    from_column(0)

    def beside_core(k):
        count(cap * width, mark((1, 0, k), 0))

    relay(1, [(beside_core, 0), (to_plane, 3), (to_plane, 1)])
    from_chips(0)
    relay(0, [(to_plane, 3), (to_plane, 1), (beside_core, 0)])
    do(*[(to_plane, k) for k in later], (from_column, 2))
    first(0)
    relay(1, [(from_column, 3)])
    second(0)
    relay(0, [(from_column, 3), (from_chips, 2), (from_column, 1)])
    relay(1, [(from_column, 1), (from_chips, 2)])
    do((first, 2))
    relay(1, [(from_chips, 3)])
    do((second, 2))
    relay(0, [(from_chips, 3)])
    relay(1, [(from_chips, 1)])
    do((to_chips, 2), (to_chips, 0), (first, 3))
    relay(0, [(from_chips, 1)])
    do((second, 3), (first, 1), (to_chips, 3), (to_column, 2), (second, 1), (to_chips, 1))
    for k in later:
        do((from_column, k), (from_chips, k), (first, k), (second, k), (to_chips, k))
    do((to_column, 3))
    early[3].wait()
    probs = lax.dot_general(
        normed, router[0], (((1,), (1,)), ((), ())), preferred_element_type=F32
    )
    probs = jnp.exp(probs - jnp.max(probs, axis=-1, keepdims=True))
    probs = probs / jnp.sum(probs, axis=-1, keepdims=True)
    prob_first = jnp.sum(probs * first_hot, axis=-1, keepdims=True)
    prob_second = jnp.sum(probs * second_hot, axis=-1, keepdims=True)
    gate = (prob_first * first_hot + prob_second * second_hot) / (prob_first + prob_second)
    combine = jnp.zeros((tok, lanes), F32)
    for k in range(experts):
        combine = combine + jnp.where(expert_of == k, gate[:, k : k + 1], 0.0)
    combine = (combine * placing)[:, 0:n_slots]
    high = combine.astype(BF)
    low = (combine - high.astype(F32)).astype(BF)

    do((to_column, 1))
    early[4].wait()
    learner_in = student[0]
    shifted = learner_in - jnp.max(learner_in, axis=-1, keepdims=True)
    learner = shifted - jnp.log(jnp.sum(jnp.exp(shifted), axis=-1, keepdims=True))
    target_col = column(targets[0:1, :])
    vocab = student.shape[2]
    picked = lax.broadcasted_iota(jnp.int32, (tok, vocab), 1).astype(F32) == target_col
    hit = jnp.sum(jnp.where(picked, learner, 0.0), axis=-1, keepdims=True)
    loads[2].wait()

    to_column(0)
    for k in later:
        to_column(k)

    for h in range(2):
        part = halves[h]
        for k in hop_order:
            count(cap * half_width, rz_r.at[2 * k + h])
            z_all[k * main : (k + 1) * main, part] = z_a[k, :, part]
            z_stage[k * rest : (k + 1) * rest, part] = z_b[k, :, part].astype(F32)
        z_all[n_main:, part] = z_stage[:, part].astype(BF)
        back = z_all[:, part]
        moe = jnp.dot(high, back, preferred_element_type=F32) + jnp.dot(
            low, back, preferred_element_type=F32
        )
        out_stage[:, part] = (mid[:, part] + moe).astype(BF)
    out = out_stage[...]
    out_copy = pltpu.make_async_copy(out_stage, layer_out.at[0], wsem.at[8])
    out_copy.start()

    final = layer_norm(out.astype(F32), gains[2]).astype(BF)
    logits = jnp.dot(final, short[...], preferred_element_type=F32)
    logits = logits - jnp.max(logits, axis=-1, keepdims=True)
    teacher = logits - jnp.log(jnp.sum(jnp.exp(logits), axis=-1, keepdims=True))
    token_loss = jnp.sum(jnp.exp(teacher) * (teacher - learner), axis=-1, keepdims=True) - hit
    counted = jnp.where(is_decoder, valid, 0.0)
    loss_sum = jnp.sum(token_loss * counted, axis=0, keepdims=True)
    loss_count = jnp.sum(counted, axis=0, keepdims=True)
    spot = lax.broadcasted_iota(jnp.int32, lsend.shape, 1)
    pair = jnp.where(spot == 0, loss_sum, jnp.where(spot == 1, loss_count, 0.0))
    lsend[...] = pair

    mine = (seg - half_seg) * n_exp + me
    n_loss = (n_seg - half_seg) * n_exp

    @pl.when(is_decoder)
    def _():
        lrecv[mine] = pair
        for ds in reversed(range(n_seg)):
            for d in range(n_exp):
                if ds or d:
                    pltpu.make_async_remote_copy(
                        lsend, lrecv.at[mine], l_s, l_r,
                        device_id=peer(ds, d), device_id_type=MESH,
                    ).start()
        landed(lrecv.at[0 : n_loss - 1], l_r)

    @pl.when(seg < half_seg)
    def _():
        landed(lrecv, l_r)

    total = lrecv[0]
    for i in range(1, (n_seg - half_seg) * n_exp):
        total = total + lrecv[i]
    loss_out[...] = total[0:1, 0:1] / total[0:1, 1:2]

    @pl.when(is_decoder)
    def _():
        landed(lwide.at[0 : n_seg * n_exp - 1], l_s)

    out_copy.wait()
    moved = 2 * cap * (experts - 1 + (2 * gx - 1) * experts)
    left = moved * width // units
    while left:
        step = min(left, win.shape[0])
        landed(win.at[0:step], sent)
        left -= step

    @pl.when(seg < half_seg)
    def _():
        landed(kmem, msem.at[2])
        len_copy.wait_send()


def local(
    hidden, memory, lengths, memory_lengths, routes, norm_gain, router,
    w_in, w_out, shortlist, student, targets,
):
    n_seg = lax.axis_size("segment")
    n_exp = lax.axis_size("expert")
    experts = router.shape[2]
    group = n_exp // experts
    gc = 2
    gx = group // gc
    tok, width = hidden.shape[1], hidden.shape[2]
    units = w_in.shape[2]
    vocab = shortlist.shape[2]
    cap = 5 * tok // 8
    main = cap // 16 * 16
    rest = cap - main
    blocks = gx * experts
    vm = pl.BlockSpec(memory_space=pltpu.VMEM)
    hbm = pl.BlockSpec(memory_space=pl.ANY)
    v = pltpu.VMEM
    dma = pltpu.SemaphoreType.DMA
    nx = max(gx - 1, 1) * experts
    scratch = [
        v((1, tok, width), BF), v((1, 2, tok), jnp.int32), v((3, 1, width), F32),
        v((1, experts, width), BF), v((1, tok, vocab), F32), v((tok, width), BF),
        v((width, units), BF), v((units, width), BF), v((width, vocab), BF),
        v((tok, width), BF), v((8, 128), jnp.int32), v((8, 128), jnp.int32), v((tok, width), F32),
        v((experts, main, width), BF), v((experts, rest, width), BF),
        v((experts * gc * gx * cap, width), BF), v((gc * blocks, rest, width), BF),
        v((gx * rest, width), F32), v((experts, gc * gx * cap, units), BF),
        v((experts, gx * cap, width), F32),
        v((experts, gx * cap, width), BF), v((experts, gx * cap, width), BF),
        v((nx, main, width), BF), v((nx, rest, width), BF),
        v((nx, main, width), BF), v((nx, rest, width), BF),
        v((experts, main, width), BF), v((experts, rest, width), BF),
        v((experts, main, width), BF), v((experts, rest, width), BF),
        v((experts * cap, width), BF), v((experts * rest, width), F32),
        v((1, 128), F32), v(((n_seg - n_seg // 2) * n_exp, 1, 128), F32),
        v((n_seg * n_exp, 1, 128), F32), v((gx * cap * width // 1024, 8, 128), BF),
        dma((9,)), dma((5,)), dma((blocks,)), dma((experts + 1,)),
        dma((2 * experts,)), dma((2 * nx,)), dma((2 * experts,)),
        dma(()), dma(()), dma(()), pltpu.SemaphoreType.REGULAR((max(experts - 2, 1),)),
    ]
    layer_out, loss = pl.pallas_call(
        functools.partial(kernel, n_seg, n_exp, experts, gx, gc),
        out_shape=(
            jax.ShapeDtypeStruct((1, tok, width), BF),
            jax.ShapeDtypeStruct((1, 1), F32),
        ),
        in_specs=[hbm, hbm, vm, vm, hbm, hbm, hbm, hbm, hbm, hbm, hbm, vm],
        out_specs=(hbm, vm),
        scratch_shapes=scratch,
        compiler_params=pltpu.CompilerParams(
            collective_id=0, has_side_effects=True, vmem_limit_bytes=60 * 1024 * 1024
        ),
    )(
        hidden, memory, lengths, memory_lengths, jnp.swapaxes(routes, 1, 2),
        jnp.swapaxes(norm_gain, 0, 1), jnp.swapaxes(router, 1, 2),
        w_in, w_out, shortlist, student, targets,
    )
    return layer_out, loss[0, 0]


def solution(mesh):
    placed = (
        P("segment", "expert", None),
        P("segment", "expert", None),
        P("segment", "expert"),
        P("segment", "expert"),
        P("segment", "expert", None),
        P("segment", None, None),
        P("segment", None, None),
        P("segment", None, "expert"),
        P("segment", "expert", None),
        P("segment", None, None),
        P("segment", "expert", None),
        P("segment", "expert"),
    )
    return jax.shard_map(
        local,
        mesh=mesh,
        in_specs=placed,
        out_specs=(P("segment", "expert", None), P()),
        check_vma=False,
    )
```
